128 devices in a mesh: lon: 16 (over z, x_lo, core), lat: 8 (over x_hi, y).
Axes of the slice: x: 4 (x_hi: 2, x_lo: 2; x = x_hi * 2 + x_lo), y: 4, z: 4, core: 2. Of those that a mesh axis runs over, the one named last changes fastest.
Arguments:
- ocean_seed: float32 [4, 10, 1024, 4096], P(None, None, 'lat', 'lon'), may hold values from -6 to 6
- forcing_pert: float32 [4, 256, 2048], P(None, 'lat', 'lon'), may hold values from -6 to 6
- land_mask: int32 [1024, 4096], P('lat', 'lon'), may hold values 0 or 1
- east_coef: float32 [1024, 4096], P('lat', 'lon'), may hold values from 0.02 to 0.2
- north_coef: float32 [1024, 4096], P('lat', 'lon'), may hold values from 0.02 to 0.2
- vert_coef: float32 [9], replicated, may hold values from 0.05 to 0.2
- remap_weight: float32 [2, 1024, 4096], P(None, 'lat', 'lon'), may hold values from 0.1 to 0.9
- ocean_slots: int32 [2, 1024, 4096], P(None, 'lat', 'lon'), may hold values from 0 to 4351, as said below
- serve_cells: int32 [8, 69632], P('lat', 'lon'), may hold values from 0 to 4095, as said below
- fold_map: int32 [4096], replicated, may hold values from 0 to 4095, as said below
Outputs:
- ocean_adjoint: float32 [4, 10, 1024, 4096], P(None, None, 'lat', 'lon')
- stress_sens: float32 [4, 256, 2048], P(None, 'lat', 'lon')
The draws below stay inside these ranges and needn't reach their ends.
Inputs may be any that keep to these rules, and one draw needn't show every extreme that they name: `ocean_slots`: a slot q < 128 is used only by ocean tiles with a > 0, a slot q >= 4224 only by tiles with a < 7. `serve_cells`: in each list, slots 0 to 127 hold cells of the band's first forcing row, slots 128 + 4096 to 4351 cells of its last forcing row. fold_map[x] = (S - 1 - x) mod 4096 for one S that is a multiple of 256.
All inputs are finite; a program needn't handle non-finite values. No bound on the sum of `land_mask` on one device may be relied on, other than what follows from the above.
Results may differ from the reference program's by a relative error of at most 0.000092.
Values sent between devices are 32-bit elements; how exact they have to be, the bound alone decides.
No kernel may reach another device: no remote copies, remote signals or barrier semaphores. Data moves between devices by JAX's collectives and lax.ppermute only.
A program may use at most 128 MiB of HBM per device.

```python
import math
import jax
import jax.numpy as jnp
from jax import lax

P_SIZE = 4
LEV = 10
K = 2
CLAT = 128
CLON = 256
FROWS = 32
FLON = 128
NY = 1024
NX = 4096
NYF = 256
NXF = 2048
FCELLS = 4096
CAP = 4352
N_LON = 16
N_LAT = 8


def draw_ocean_seed(key, part):
    base = jax.random.normal(key, (P_SIZE, LEV, NY, NX), jnp.float32)
    return jnp.clip(base, -6.0, 6.0)


def permute_many(key, count, length):
    keys = jax.random.split(key, count)
    return jax.vmap(lambda single: jax.random.permutation(single, length))(keys).astype(jnp.int32)


def remap_tables(key):
    bands = NY // CLAT
    pieces = NX // CLON
    own_list = permute_many(jax.random.fold_in(key, 21), bands * pieces, FCELLS).reshape(bands, pieces, FCELLS)
    lower_list = permute_many(jax.random.fold_in(key, 22), bands * pieces, FLON).reshape(bands, pieces, FLON)
    upper_list = permute_many(jax.random.fold_in(key, 23), bands * pieces, FLON).reshape(bands, pieces, FLON)
    return (own_list, lower_list, upper_list)


def draw_serve_cells(key, part):
    own_list, lower_list, upper_list = remap_tables(key)
    bands = NY // CLAT
    pieces = NX // CLON
    whole = jnp.concatenate([lower_list, own_list, (FROWS - 1) * FLON + upper_list], axis=-1)
    return whole.reshape(bands, pieces * CAP).astype(jnp.int32)


def draw_ocean_slots(key, part):
    own_list, lower_list, upper_list = remap_tables(key)
    bands = NY // CLAT
    own_inverse = jnp.argsort(own_list, axis=-1).astype(jnp.int32)
    lower_inverse = jnp.argsort(lower_list, axis=-1).astype(jnp.int32)
    upper_inverse = jnp.argsort(upper_list, axis=-1).astype(jnp.int32)
    rows = jnp.arange(NY, dtype=jnp.int32)[:, None]
    cols = jnp.arange(NX, dtype=jnp.int32)[None, :]
    tile_lat = jnp.broadcast_to(rows // CLAT, (NY, NX))
    tile_lon = jnp.broadcast_to(cols // CLON, (NY, NX))
    local_row = jnp.broadcast_to(rows % CLAT, (NY, NX))
    local_col = jnp.broadcast_to(cols % CLON, (NY, NX))
    frow = local_row * FROWS // CLAT
    fcol = local_col * FLON // CLON
    first = FLON + own_inverse[tile_lat, tile_lon, frow * FLON + fcol]
    heading = jax.random.randint(jax.random.fold_in(key, 31), (NY, NX), 0, 4)
    frow_two = jnp.clip(frow + (heading == 0).astype(jnp.int32) - (heading == 1).astype(jnp.int32), 0, FROWS - 1)
    fcol_two = jnp.clip(fcol + (heading == 2).astype(jnp.int32) - (heading == 3).astype(jnp.int32), 0, FLON - 1)
    second = FLON + own_inverse[tile_lat, tile_lon, frow_two * FLON + fcol_two]
    below = upper_inverse[jnp.clip(tile_lat - 1, 0, bands - 1), tile_lon, fcol]
    above = FLON + FCELLS + lower_inverse[jnp.clip(tile_lat + 1, 0, bands - 1), tile_lon, fcol]
    second = jnp.where((local_row == 0) & (tile_lat > 0), below, second)
    second = jnp.where((local_row == CLAT - 1) & (tile_lat < bands - 1), above, second)
    return jnp.stack([first, second]).astype(jnp.int32)


def draw_fold_map(key, part):
    shift = CLON * jax.random.randint(jax.random.fold_in(key, 41), (), 0, NX // CLON)
    return ((shift - 1 - jnp.arange(NX, dtype=jnp.int32)) % NX).astype(jnp.int32)


def plant(result, rng, smallest, high):
    longest = result.shape.index(max(result.shape))
    spots = []
    for shift in (0, 1):
        where = [jax.random.randint(jax.random.fold_in(rng, axis), (), 0, length) for axis, length in enumerate(result.shape)]
        where[longest] = (where[longest] + shift) % result.shape[longest]
        spots.append(tuple(where))
    return result.at[spots[0]].set(smallest).at[spots[1]].set(high)


def steps_of(key, extent, cuts, smallest, top_value):
    factor_of = 1.0
    for dim, shards_of in cuts:
        steps = jax.random.uniform(jax.random.fold_in(jax.random.fold_in(key, 6), dim), (shards_of,), jnp.float32, smallest / len(cuts), top_value / len(cuts))
        factor_of = factor_of * jnp.repeat(jnp.exp(steps), extent[dim] // shards_of).reshape((-1,) + (1,) * (len(extent) - 1 - dim))
    return factor_of


def normal_values(stream_key, shape, deviation, bound, cuts=(), kind=jnp.bfloat16):
    drawn = jax.random.normal(stream_key, shape, jnp.float32) * deviation
    if len(cuts) > 0:
        drawn = steps_of(stream_key, shape, cuts, -0.22, 0.18) * drawn
    return jnp.clip(drawn, min=-bound, max=bound).astype(kind)


def setup_inputs(seed: int = 0) -> dict:
    streams_of = jax.random.split(jax.random.key(seed), 11)
    ocean_seed = draw_ocean_seed(jax.random.fold_in(streams_of[10], 71), 0)
    forcing_pert = normal_values(streams_of[1], (P_SIZE, NYF, NXF), 1.0, 6.0, ((1, 8), (2, 16)), jnp.float32)
    land_mask = plant((jax.random.randint(streams_of[2], (NY, NX), 0, 4) < 3).astype(jnp.int32), jax.random.fold_in(streams_of[2], 1), 0, 1)
    east_coef = jnp.clip(jnp.exp(math.log(0.2) - 2.3025851 * jax.random.uniform(streams_of[3], (NY, NX), jnp.float32) ** steps_of(streams_of[3], (NY, NX), ((0, 8), (1, 16)), -0.2, 0.2)), 0.02, 0.2)
    north_coef = jnp.clip(jnp.exp(math.log(0.2) - 2.3025851 * jax.random.uniform(streams_of[4], (NY, NX), jnp.float32) ** steps_of(streams_of[4], (NY, NX), ((0, 8), (1, 16)), -0.2, 0.2)), 0.02, 0.2)
    vert_coef = jnp.clip(jnp.exp(jax.random.uniform(streams_of[5], (LEV - 1,), jnp.float32, math.log(0.05), math.log(0.2))), 0.05, 0.2)
    remap_weight = jnp.clip(0.1 + 0.79999997 * jax.random.uniform(streams_of[6], (K, NY, NX), jnp.float32) ** steps_of(streams_of[6], (K, NY, NX), ((1, 8), (2, 16)), -0.2, 0.2), 0.1, 0.9)
    ocean_slots = draw_ocean_slots(jax.random.fold_in(streams_of[10], 71), 0)
    serve_cells = draw_serve_cells(jax.random.fold_in(streams_of[10], 71), 0)
    fold_map = draw_fold_map(jax.random.fold_in(streams_of[10], 71), 0)
    return {"ocean_seed": ocean_seed, "forcing_pert": forcing_pert, "land_mask": land_mask, "east_coef": east_coef, "north_coef": north_coef, "vert_coef": vert_coef, "remap_weight": remap_weight, "ocean_slots": ocean_slots, "serve_cells": serve_cells, "fold_map": fold_map}


def advance_plane(adjoint, east_coef, north_coef, wet_mask, vert_coef, fold_map):
    eastward = jnp.roll(adjoint, -1, axis=2)
    westward = jnp.roll(adjoint, 1, axis=2)
    fold_row = adjoint[:, -1:, :][:, :, fold_map]
    northward = jnp.concatenate([adjoint[:, 1:], fold_row], axis=1)
    southward = jnp.concatenate([jnp.zeros_like(adjoint[:, :1]), adjoint[:, :-1]], axis=1)
    west_face = jnp.roll(east_coef, 1, axis=1)
    south_face = jnp.concatenate([jnp.zeros_like(north_coef[:1]), north_coef[:-1]], axis=0)
    lateral = east_coef * (eastward - adjoint) + west_face * (westward - adjoint) + north_coef * (northward - adjoint) + south_face * (southward - adjoint)
    vertical_flux = vert_coef[:, None, None] * (adjoint[1:] - adjoint[:-1])
    zero_level = jnp.zeros_like(adjoint[:1])
    vertical = jnp.concatenate([vertical_flux, zero_level], 0) - jnp.concatenate([zero_level, vertical_flux], 0)
    return wet_mask * (adjoint + lateral + vertical)


def slot_source(slots, tile_lat):
    side = (slots >= FLON).astype(jnp.int32) + (slots >= FLON + FCELLS).astype(jnp.int32) - 1
    band = jnp.clip(tile_lat + side, 0, N_LAT - 1)
    position = slots - side * (FCELLS + FLON)
    return band, position


def reference(ocean_seed, forcing_pert, land_mask, east_coef, north_coef, vert_coef, remap_weight, ocean_slots, serve_cells, fold_map):
    wet_mask = land_mask.astype(jnp.float32)
    band_grid = jnp.arange(N_LAT, dtype=jnp.int32)[:, None, None]
    lon_grid = jnp.arange(N_LON, dtype=jnp.int32)[None, :, None]
    served = serve_cells.reshape(N_LAT, N_LON, CAP)
    forcing_row = band_grid * FROWS + served // FLON
    forcing_col = lon_grid * FLON + served % FLON
    looked_up = forcing_pert[:, forcing_row, forcing_col]
    tile_lat = (jnp.arange(NY, dtype=jnp.int32) // CLAT)[None, :, None]
    tile_lon = (jnp.arange(NX, dtype=jnp.int32) // CLON)[None, None, :]
    band_index, position = slot_source(ocean_slots, tile_lat)
    picked = looked_up[:, band_index, tile_lon, position]
    surface_image = jnp.sum(remap_weight[None] * picked, axis=1)
    adjoint_start = ocean_seed.at[:, 0].add(surface_image)

    def stepper(plane):
        return advance_plane(plane, east_coef, north_coef, wet_mask, vert_coef, fold_map)

    adjoint_one = lax.map(stepper, adjoint_start)
    adjoint_two = lax.map(stepper, adjoint_one)
    surface_sum = adjoint_one[:, 0] + adjoint_two[:, 0]
    segment = ((tile_lat * N_LON + tile_lon) * CAP + ocean_slots).reshape(-1)
    weighted = (remap_weight[None] * surface_sum[:, None]).reshape(P_SIZE, -1)
    slot_sums = jax.vmap(lambda values: jax.ops.segment_sum(values, segment, num_segments=N_LAT * N_LON * CAP))(weighted)
    slot_grid = jnp.arange(CAP, dtype=jnp.int32)[None, None, :]
    slot_band, slot_position = slot_source(slot_grid, band_grid)
    lon_full = jnp.broadcast_to(lon_grid, (N_LAT, N_LON, CAP))
    band_full = jnp.broadcast_to(slot_band, (N_LAT, N_LON, CAP))
    position_full = jnp.broadcast_to(slot_position, (N_LAT, N_LON, CAP))
    target = forcing_row[band_full, lon_full, position_full] * NXF + forcing_col[band_full, lon_full, position_full]
    stress_sens = jax.vmap(lambda values: jax.ops.segment_sum(values, target.reshape(-1), num_segments=NYF * NXF))(slot_sums)
    return adjoint_two, stress_sens.reshape(P_SIZE, NYF, NXF)
```

```python
import jax
import jax.numpy as jnp
from jax import lax
from jax.experimental import pallas as pl
from jax.experimental.pallas import tpu as pltpu
from jax.sharding import PartitionSpec as P

PL = 4
LEV = 10
ROWS = 128
COLS = 256
NPL = PL * LEV
MSG = 48
CORNER = 43
LISTS = 34
HI = 17
HPAD = 18
F32 = jnp.float32
BF16 = jnp.bfloat16
GROUPS = ROWS // 8
VM = pltpu.CompilerParams(vmem_limit_bytes=56 * 1024 * 1024)


def lane_iota(shape):
    return lax.broadcasted_iota(jnp.int32, shape, len(shape) - 1)


def row_iota(shape):
    return lax.broadcasted_iota(jnp.int32, shape, len(shape) - 2)


def lookup(row, low):
    table = jnp.broadcast_to(row, low.shape)
    return jnp.take_along_axis(table, low, axis=1, mode="promise_in_bounds")


def pick_body(
    forcing, serve, south, north, slots, weights, seed, east, north_c, land,
    surf, to_east, to_west, send_a, send_b, pool,
):
    even = lax.axis_index("lat") % 2 == 0
    step = pl.program_id(0)
    steps = pl.num_programs(0)

    @pl.when(step == 0)
    def _():
        pool[:, LISTS:, :] = jnp.zeros((PL, 40 - LISTS, 128), F32)
        for g in range(4):
            ids = jnp.concatenate(
                [serve[:, 128 * (8 * g + i + 1) : 128 * (8 * g + i + 2)] for i in range(8)], axis=0
            )
            low = ids & 127
            high = ids >> 7
            acc = [jnp.zeros((8, 128), F32) for _ in range(PL)]
            for h in range(32):
                hit = high == h
                for p in range(PL):
                    acc[p] = jnp.where(hit, lookup(forcing[p, h : h + 1, :], low), acc[p])
            for p in range(PL):
                pool[p, 1 + 8 * g : 9 + 8 * g, :] = acc[p]
        for recv, place in ((south, 0), (north, LISTS - 1)):
            low = jnp.broadcast_to(recv[4:5, :].astype(jnp.int32) & 127, (8, 128))
            for p in range(PL):
                got = lookup(recv[p : p + 1, :], low)
                pool[p, place : place + 1, :] = got[0:1, :]

    block = surf.shape[1]
    lanes = lane_iota((8, 128))
    for g in range(block // 8):
        rs = slice(8 * g, 8 * g + 8)
        image = []
        for t in range(2):
            cs = slice(128 * t, 128 * t + 128)
            acc = []
            for k in range(2):
                ids = slots[k, rs, cs]
                low = ids & 127
                high = ids >> 7
                own = [jnp.zeros((8, 128), F32) for _ in range(PL)]
                for h in range(LISTS):
                    hit = high == h
                    for p in range(PL):
                        own[p] = jnp.where(hit, lookup(pool[p, h : h + 1, :], low), own[p])
                acc.append(own)
            image.append(
                [weights[0, rs, cs] * acc[0][p] + weights[1, rs, cs] * acc[1][p] for p in range(PL)]
            )
        for p in range(PL):
            surf[p, rs, 0:128] = image[0][p]
            surf[p, rs, 128:256] = image[1][p]
        pair = lanes >> 1
        statics = (east, north_c, land)
        for t, out, first in ((0, to_west, 0), (1, to_east, 126)):
            cs = slice(128 * t, 128 * t + 128)
            acc = jnp.zeros((8, 128), F32)
            for m in range(NPL + 3):
                if m < NPL:
                    p, k = divmod(m, LEV)
                    v = seed[p, k, rs, cs]
                    if k == 0:
                        v = v + image[t][p]
                else:
                    v = statics[m - NPL][rs, cs].astype(F32)
                shift = (2 * m - first) % 128
                if shift:
                    v = pltpu.roll(v, shift, 1)
                acc = jnp.where(pair == m, v, acc)
            out[rs, :] = acc

    def rows_out(out, adjacent, second):
        out[...] = jnp.zeros_like(out)
        for c, r in ((0, adjacent), (1, second)):
            for t in range(2):
                cs = slice(128 * t, 128 * t + 128)
                for m in range(NPL):
                    p, k = divmod(m, LEV)
                    v = seed[p, k, r : r + 1, cs]
                    if k == 0:
                        v = v + surf[p, r : r + 1, cs]
                    out[2 * c + t, m : m + 1, :] = v
                out[2 * c + t, 40:41, :] = east[r : r + 1, cs]
                out[2 * c + t, 41:42, :] = north_c[r : r + 1, cs]
                out[2 * c + t, 42:43, :] = land[r : r + 1, cs].astype(F32)

    for flag, low_out, high_out in ((even, send_b, send_a), (jnp.logical_not(even), send_a, send_b)):

        @pl.when(jnp.logical_and(flag, step == 0))
        def _():
            rows_out(low_out, 0, 1)

        @pl.when(jnp.logical_and(flag, step == steps - 1))
        def _():
            rows_out(high_out, block - 1, block - 2)


def pick(forcing, serve, south, north, slots, weights, seed, east, north_c, land):
    block = 16
    whole = lambda *shape: pl.BlockSpec(shape, lambda i: (0,) * len(shape))
    tile = pl.BlockSpec((block, COLS), lambda i: (i, 0))
    pair = pl.BlockSpec((2, block, COLS), lambda i: (0, i, 0))
    return pl.pallas_call(
        pick_body,
        grid=(ROWS // block,),
        in_specs=[
            whole(PL, 32, 128), whole(1, LISTS * 128), whole(8, 128), whole(8, 128), pair, pair,
            pl.BlockSpec((PL, LEV, block, COLS), lambda i: (0, 0, i, 0)), tile, tile, tile,
        ],
        out_specs=[
            pl.BlockSpec((PL, block, COLS), lambda i: (0, i, 0)),
            pl.BlockSpec((block, 128), lambda i: (i, 0)),
            pl.BlockSpec((block, 128), lambda i: (i, 0)),
            whole(4, MSG, 128),
            whole(4, MSG, 128),
        ],
        out_shape=[
            jax.ShapeDtypeStruct((PL, ROWS, COLS), F32),
            jax.ShapeDtypeStruct((ROWS, 128), F32),
            jax.ShapeDtypeStruct((ROWS, 128), F32),
            jax.ShapeDtypeStruct((4, MSG, 128), F32),
            jax.ShapeDtypeStruct((4, MSG, 128), F32),
        ],
        scratch_shapes=[pltpu.VMEM((PL, 40, 128), F32)],
        compiler_params=VM,
        name="pick",
    )(forcing, serve, south, north, slots, weights, seed, east, north_c, land)


def corner_body(west_first, west_last, east_first, east_last, tile_a, tile_b, out_a, out_b):
    even = lax.axis_index("lat") % 2 == 0
    odd = (lane_iota((8, 128)) & 1) == 1
    low = jnp.where(odd, west_first[0:1, :], east_first[0:1, :])
    high = jnp.where(odd, west_last[7:8, :], east_last[7:8, :])
    here = row_iota((8, 128)) == CORNER - 40
    out_a[0] = jnp.where(here, jnp.where(even, high, low), tile_a[0])
    out_b[0] = jnp.where(here, jnp.where(even, low, high), tile_b[0])


def corners(west, east, send_a, send_b):
    first = pl.BlockSpec((8, 128), lambda i: (0, 0))
    last = pl.BlockSpec((8, 128), lambda i: (GROUPS - 1, 0))
    spot = pl.BlockSpec((1, 8, 128), lambda i: (0, 5, 0))
    message = jax.ShapeDtypeStruct((4, MSG, 128), F32)
    return pl.pallas_call(
        corner_body,
        grid=(1,),
        in_specs=[first, last, first, last, spot, spot],
        out_specs=[spot, spot],
        out_shape=[message, message],
        input_output_aliases={4: 0, 5: 1},
        name="corners",
    )(west, west, east, east, send_a, send_b)


def ring(
    vert, to_east, to_west, west, east, send_a, send_b, got_a, got_b,
    rows_south, rows_north, rows_south1, rows_north1, west1, east1,
):
    place = lax.axis_index("lat")
    even = place % 2 == 0
    fold = place == lax.axis_size("lat") - 1
    lanes = lane_iota((1, 128))
    odd = (lanes & 1) == 1

    def chosen(flag, yes, no):
        return jnp.where(flag, yes, no)

    a = got_a[...]
    b = got_b[...]
    above = chosen(even, a, b)
    below = chosen(even, b, a)
    top = chosen(even, send_a[...], send_b[...])
    bottom = chosen(even, send_b[...], send_a[...])
    back = 127 - lane_iota((MSG, 128))
    flip = lambda x: jnp.take_along_axis(x, back, axis=1, mode="promise_in_bounds")
    turned = [flip(above[1]), flip(above[0]), flip(above[3]), flip(above[2])]
    corner_above = above[0, CORNER : CORNER + 1, :]
    corner_below = below[0, CORNER : CORNER + 1, :]
    swapped = jnp.where(odd, pltpu.roll(corner_above, 1, 1), pltpu.roll(corner_above, 127, 1))
    pick_lane = lambda x, lane: jnp.sum(jnp.where(lane_iota(x.shape) == lane, x, 0.0), axis=1, keepdims=True)
    e_above = jnp.concatenate([above[0, 40:41, :], above[1, 40:41, :]], axis=1)
    e_turn = jnp.concatenate([turned[0][40:41, :], turned[1][40:41, :]], axis=1)
    wide = lane_iota((1, COLS))
    e_edge = pick_lane(corner_above, 81)
    e_fold = jnp.where(wide == 255, e_edge, pltpu.roll(e_turn, 255, 1))
    e_fold_west = e_turn[:, 0:1]

    n0 = jnp.concatenate([chosen(fold, turned[0], above[0]), chosen(fold, turned[1], above[1])], axis=1)
    n1 = jnp.concatenate([chosen(fold, turned[2], above[2]), chosen(fold, turned[3], above[3])], axis=1)
    s0 = jnp.concatenate([below[0], below[1]], axis=1)
    s1 = jnp.concatenate([below[2], below[3]], axis=1)
    own_top = jnp.concatenate([top[0], top[1]], axis=1)
    own_bottom = jnp.concatenate([bottom[0], bottom[1]], axis=1)
    corner_n = chosen(fold, swapped, corner_above)
    e_n = chosen(fold, e_fold, e_above)
    e_n_west = chosen(fold, e_fold_west, e_edge)
    toward_n = chosen(fold, n0[41:42, :], own_top[41:42, :])
    away_n = chosen(fold, n1[41:42, :], n0[41:42, :])

    def level_coefs(plane):
        level = plane % LEV
        upper = jnp.zeros(plane.shape, F32)
        lower = jnp.zeros(plane.shape, F32)
        for k in range(LEV - 1):
            upper = jnp.where(level == k, vert[k], upper)
            lower = jnp.where(level == k + 1, vert[k], lower)
        return upper, lower

    row_up, row_down = level_coefs(row_iota((MSG, COLS)))

    def row_step(cur, toward, away, toward_c, away_c, e_row, e_west, corner):
        spread = jnp.broadcast_to(corner, (MSG, 128))
        where = lane_iota((MSG, 128))
        plane = row_iota((MSG, 128))
        from_west = jnp.sum(jnp.where(where == 2 * plane + 1, spread, 0.0), axis=1, keepdims=True)
        from_east = jnp.sum(jnp.where(where == 2 * plane, spread, 0.0), axis=1, keepdims=True)
        lane = lane_iota((MSG, COLS))
        east_u = jnp.where(lane == COLS - 1, from_east, pltpu.roll(cur, COLS - 1, 1))
        west_u = jnp.where(lane == 0, from_west, pltpu.roll(cur, 1, 1))
        e_left = jnp.where(wide == 0, e_west, pltpu.roll(e_row, 1, 1))
        up = pltpu.roll(cur, MSG - 1, 0)
        down = pltpu.roll(cur, 1, 0)
        wet = cur[42:43, :]
        return wet * (
            cur
            + e_row * (east_u - cur)
            + e_left * (west_u - cur)
            + toward_c * (toward - cur)
            + away_c * (away - cur)
            + row_up * (up - cur)
            + row_down * (down - cur)
        )

    n_first = row_step(n0, own_top, n1, toward_n, away_n, e_n, e_n_west, corner_n)
    s_first = row_step(
        s0, own_bottom, s1, s0[41:42, :], s1[41:42, :], s0[40:41, :], pick_lane(corner_below, 81), corner_below
    )
    rows_north[...] = n0
    rows_south[...] = s0
    rows_north1[...] = n_first
    rows_south1[...] = s_first

    shape = (ROWS, 128)
    lane = lane_iota(shape)
    row = row_iota(shape)
    col_up, col_down = level_coefs(lane_iota((1, 128)) >> 1)

    def col_step(cur, east_u, west_u, e_right, e_left, n_col, n_south, wet):
        north_u = jnp.where(row == ROWS - 1, corner_n, pltpu.roll(cur, ROWS - 1, 0))
        south_u = jnp.where(row == 0, corner_below, pltpu.roll(cur, 1, 0))
        n_below = jnp.where(row_iota((ROWS, 1)) == 0, n_south, pltpu.roll(jnp.broadcast_to(n_col, shape), 1, 0))
        return wet * (
            cur
            + e_right * (east_u - cur)
            + e_left * (west_u - cur)
            + n_col * (north_u - cur)
            + n_below * (south_u - cur)
            + col_up * (pltpu.roll(cur, 126, 1) - cur)
            + col_down * (pltpu.roll(cur, 2, 1) - cur)
        )

    w = west[...]
    e = east[...]
    mine_w = to_west[...]
    mine_e = to_east[...]
    lane_of = lambda x, n: x[:, n : n + 1]
    west1[...] = col_step(
        w, pltpu.roll(mine_w, 1, 1), pltpu.roll(w, 1, 1), lane_of(w, 81), lane_of(w, 80),
        lane_of(w, 83), pick_lane(corner_below, 83), lane_of(w, 85),
    )
    east1[...] = col_step(
        e, pltpu.roll(e, 127, 1), pltpu.roll(mine_e, 127, 1), lane_of(e, 80), lane_of(mine_e, 81),
        lane_of(e, 82), pick_lane(corner_below, 82), lane_of(e, 84),
    )


def step_body(
    vert, seed, surf, east, north, land, to_east, to_west, west0, east0, send_a, send_b, got_a, got_b,
    out, total, start, first, coef, side, west1, east1, south0, north0, south1, north1,
):
    p = pl.program_id(0)

    @pl.when(p == 0)
    def _():
        ring(
            vert, to_east, to_west, west0, east0, send_a, send_b, got_a, got_b,
            south0, north0, south1, north1, west1, east1,
        )

    @pl.when(p == 0)
    def _():
        wide = lane_iota((ROWS, COLS))
        tall = row_iota((ROWS, COLS))
        e = east[...]
        n = north[...]
        wet = land[...].astype(F32)
        e_left = jnp.where(wide == 0, west0[:, 81:82], pltpu.roll(e, 1, 1))
        n_below = jnp.where(tall == 0, south0[41:42, :], pltpu.roll(n, 1, 0))
        coef[0] = wet * e
        coef[1] = wet * e_left
        coef[2] = wet * n
        coef[3] = wet * n_below
        coef[4] = wet - wet * (e + e_left + n + n_below)
        coef[5] = wet

    turn = 128 - 2 * LEV * p
    odd = (lane_iota((ROWS, 128)) & 1) == 1
    for i, w, e in ((0, west0, east0), (1, west1, east1)):
        pack = pltpu.roll(jnp.where(odd, w[...], pltpu.roll(e[...], 2, 1)), turn, 1)
        for k in range(LEV):
            side[i, k] = pltpu.roll(pack, 126 - 2 * k, 1)
    for k in range(LEV):
        start[k, 7:8, :] = south0[pl.ds(p * LEV + k, 1), :]
        start[k, 136:137, :] = north0[pl.ds(p * LEV + k, 1), :]
        first[k, 7:8, :] = south1[pl.ds(p * LEV + k, 1), :]
        first[k, 136:137, :] = north1[pl.ds(p * LEV + k, 1), :]
        block = seed[0, k]
        if k == 0:
            block = block + surf[0]
        start[k, 8:136, :] = block

    lane = lane_iota((8, 128))
    sub = row_iota((8, 128))

    def advance(src, edge_at, store):
        def group(g, carry):
            row = pl.multiple_of(g * 8, 8)
            here = pl.ds(row + 8, 8)
            cs = [slice(0, 128), slice(128, 256)]
            c = [[coef[i, pl.ds(row, 8), cs[t]] for t in range(2)] for i in range(6)]
            below = [None, None]
            u = [src[0, here, cs[t]] for t in range(2)]
            for k in range(LEV):
                edge = side[edge_at, k, pl.ds(row, 8), :]
                east_of = [jnp.where(lane == 0, u[1], u[0]), jnp.where(lane == 0, edge, u[1])]
                west_of = [jnp.where(lane == 127, edge, u[0]), jnp.where(lane == 127, u[0], u[1])]
                ahead = [None, None]
                for t in range(2):
                    up_rows = src[k, pl.ds(row + 16, 8), cs[t]]
                    dn_rows = src[k, pl.ds(row, 8), cs[t]]
                    north_u = pltpu.roll(jnp.where(sub == 0, up_rows, u[t]), 7, 0)
                    south_u = pltpu.roll(jnp.where(sub == 7, dn_rows, u[t]), 1, 0)
                    east_u = pltpu.roll(east_of[t], 127, 1)
                    west_u = pltpu.roll(west_of[t], 1, 1)
                    new = (
                        c[4][t] * u[t]
                        + c[0][t] * east_u
                        + c[1][t] * west_u
                        + c[2][t] * north_u
                        + c[3][t] * south_u
                    )
                    flux = None
                    if k + 1 < LEV:
                        ahead[t] = src[k + 1, here, cs[t]]
                        flux = vert[k] * (ahead[t] - u[t])
                    if flux is None:
                        new = new - c[5][t] * below[t]
                    elif below[t] is None:
                        new = new + c[5][t] * flux
                    else:
                        new = new + c[5][t] * (flux - below[t])
                    below[t] = flux
                    store(k, row, cs[t], new)
                u = ahead
            return carry

        lax.fori_loop(0, GROUPS, group, 0, unroll=4)

    def keep(k, row, cs, new):
        first[k, pl.ds(row + 8, 8), cs] = new

    def finish(k, row, cs, new):
        out[0, k, pl.ds(row, 8), cs] = new
        if k == 0:
            total[0, pl.ds(row, 8), cs] = new + first[0, pl.ds(row + 8, 8), cs]

    advance(start, 0, keep)
    advance(first, 1, finish)


def steps(vert, seed, surf, east, north, land, to_east, to_west, west, east_in, send_a, send_b, got_a, got_b):
    whole = lambda *shape: pl.BlockSpec(shape, lambda i: (0,) * len(shape))
    tile = whole(ROWS, COLS)
    cols = whole(ROWS, 128)
    message = whole(4, MSG, 128)
    plane = pl.BlockSpec((1, ROWS, COLS), lambda i: (i, 0, 0))
    stack = pl.BlockSpec((1, LEV, ROWS, COLS), lambda i: (i, 0, 0, 0))
    return pl.pallas_call(
        step_body,
        grid=(PL,),
        in_specs=[pl.BlockSpec(memory_space=pltpu.SMEM), stack, plane, tile, tile, tile]
        + [cols] * 4
        + [message] * 4,
        out_specs=[stack, plane],
        out_shape=[
            jax.ShapeDtypeStruct((PL, LEV, ROWS, COLS), F32),
            jax.ShapeDtypeStruct((PL, ROWS, COLS), F32),
        ],
        scratch_shapes=[
            pltpu.VMEM((LEV, ROWS + 16, COLS), F32),
            pltpu.VMEM((LEV, ROWS + 16, COLS), F32),
            pltpu.VMEM((6, ROWS, COLS), F32),
            pltpu.VMEM((2, LEV, ROWS, 128), F32),
            pltpu.VMEM((ROWS, 128), F32),
            pltpu.VMEM((ROWS, 128), F32),
            pltpu.VMEM((MSG, COLS), F32),
            pltpu.VMEM((MSG, COLS), F32),
            pltpu.VMEM((MSG, COLS), F32),
            pltpu.VMEM((MSG, COLS), F32),
        ],
        compiler_params=VM,
        name="steps",
    )(vert, seed, surf, east, north, land, to_east, to_west, west, east_in, send_a, send_b, got_a, got_b)


def hot_low(ids):
    grid = row_iota((COLS, ids.shape[1]))
    return jnp.where(grid == (ids & 255), 1.0, 0.0).astype(BF16)


def hot_high(ids, parts, count):
    high = jnp.broadcast_to(ids >> 8, parts.shape)
    return jnp.concatenate([jnp.where(high == h, parts, 0.0) for h in range(count)], axis=0).astype(BF16)


def two_parts(values):
    big = values.astype(BF16).astype(F32)
    return jnp.concatenate([big, values - big], axis=0)


CONTRACT = (((1,), (1,)), ((), ()))


def spread_body(total, weights, slots, sums, to_north, to_south, grid_low):
    grid_low[...] = row_iota((COLS, COLS)).astype(F32).astype(BF16)
    which = (row_iota((16, COLS)) >> 3).astype(F32)
    pairs = HPAD // 2

    def accumulate(acc0, acc1):
        accs = (acc0, acc1)

        def block(i, carry):
            rows = pl.ds(pl.multiple_of(i * 8, 8), 8)
            ids_all = [slots[k, rows, :] for k in range(2)]
            w_all = [weights[k, rows, :] for k in range(2)]
            t_all = [total[p, rows, :] for p in range(PL)]
            unit = 0
            for r in range(8):
                surface = jnp.concatenate([t[r : r + 1, :] for t in t_all], axis=0)
                for k in range(2):
                    ids = ids_all[k][r : r + 1, :]
                    low = jnp.broadcast_to((ids & 255).astype(F32), (16, COLS)).astype(BF16)
                    low = jnp.concatenate([low] * 16, axis=0)
                    one_hot = jnp.where(grid_low[...] == low, jnp.array(1, BF16), jnp.array(0, BF16))
                    parts = two_parts(surface * w_all[k][r : r + 1, :])
                    parts = jnp.concatenate([parts, parts], axis=0).astype(BF16)
                    high = jnp.broadcast_to((ids >> 8).astype(F32), (16, COLS)) - which
                    high = high.astype(BF16)
                    hot = jnp.concatenate(
                        [jnp.where(high == jnp.array(2 * h, BF16), parts, jnp.array(0, BF16)) for h in range(pairs)],
                        axis=0,
                    )
                    m = unit % 2
                    reg = (unit // 2) % 2
                    pltpu.matmul_push_rhs(one_hot, reg, m, transpose=True)
                    pltpu.matmul_acc_lhs(accs[m], hot, load_staged_rhs=reg)
                    unit += 1
            return carry

        lax.fori_loop(0, GROUPS, block, 0)
        summed = pltpu.matmul_pop(acc0) + pltpu.matmul_pop(acc1)
        sums[...] = summed
        to_north[...] = summed[128:136, 128:] + pltpu.roll(summed[128:136, 128:], 4, 0)
        to_south[...] = summed[0:8, :128] + pltpu.roll(summed[0:8, :128], 4, 0)

    pl.run_scoped(accumulate, *[pltpu.ACC(m)((HPAD * 8, COLS), F32) for m in range(2)])


def spread(total, weights, slots):
    whole = lambda *shape: pl.BlockSpec(shape, lambda i: (0,) * len(shape))
    small = jax.ShapeDtypeStruct((8, 128), F32)
    return pl.pallas_call(
        spread_body,
        grid=(1,),
        in_specs=[whole(PL, ROWS, COLS), whole(2, ROWS, COLS), whole(2, ROWS, COLS)],
        out_specs=[whole(HPAD * 8, COLS), whole(8, 128), whole(8, 128)],
        out_shape=[jax.ShapeDtypeStruct((HPAD * 8, COLS), F32), small, small],
        scratch_shapes=[pltpu.VMEM((COLS, COLS), BF16)],
        compiler_params=VM,
        name="spread",
    )(total, weights, slots)


def gather_body(sums, south, north, serve, out):
    lane = lane_iota((PL, COLS))
    acc = jnp.zeros((128, COLS), F32)
    for h in range(HI):
        tile = sums[8 * h : 8 * h + 8, :]
        values = tile[0:4, :] + tile[4:8, :]
        if h == 0:
            values = jnp.where(lane < 128, jnp.concatenate([south[0:4, :], south[0:4, :]], axis=1), values)
        if h == HI - 1:
            values = jnp.where(lane >= 128, jnp.concatenate([north[0:4, :], north[0:4, :]], axis=1), values)
        ids = serve[:, COLS * h : COLS * h + COLS]
        acc = acc + lax.dot_general(
            hot_high(ids, two_parts(values), 16), hot_low(ids), CONTRACT, preferred_element_type=F32
        )
    for h in range(16):
        tile = acc[8 * h : 8 * h + 8, :]
        values = tile[0:4, :] + tile[4:8, :]
        for p in range(PL):
            for t in range(2):
                out[p, 2 * h + t : 2 * h + t + 1, :] = values[p : p + 1, 128 * t : 128 * t + 128]


def gather(sums, south, north, serve):
    whole = lambda *shape: pl.BlockSpec(shape, lambda i: (0,) * len(shape))
    return pl.pallas_call(
        gather_body,
        grid=(1,),
        in_specs=[whole(HPAD * 8, COLS), whole(8, 128), whole(8, 128), whole(1, LISTS * 128)],
        out_specs=whole(PL, 32, 128),
        out_shape=jax.ShapeDtypeStruct((PL, 32, 128), F32),
        compiler_params=VM,
        name="gather",
    )(sums, south, north, serve)


def ladder(lon_count, lat_count, shift):
    place = lambda a, j: j * lat_count + a
    pairs = []
    for j in range(lon_count):
        for a in range(1, lat_count - 1, 2):
            pairs.append((place(a, j), place(a + 1, j)))
            pairs.append((place(a + 1, j), place(a, j)))
        pairs.append((place(lat_count - 1, j), place(lat_count - 1, (shift - 1 - j) % lon_count)))
    return pairs


def shards(
    ocean_seed, forcing_pert, land_mask, east_coef, north_coef, vert_coef, remap_weight, ocean_slots,
    serve_cells, fold_map,
):
    lat_count = lax.axis_size("lat")
    lon_count = lax.axis_size("lon")
    upward = [(i, i + 1) for i in range(lat_count - 1)]
    downward = [(i + 1, i) for i in range(lat_count - 1)]
    eastward = [(i, (i + 1) % lon_count) for i in range(lon_count)]
    westward = [((i + 1) % lon_count, i) for i in range(lon_count)]

    cells = serve_cells.reshape(-1)

    def list_message(row, ids):
        return jnp.concatenate([row, ids.astype(F32)[None], jnp.zeros((3, 128), F32)], axis=0)

    south_list = lax.ppermute(list_message(forcing_pert[:, -1], cells[-128:]), "lat", upward)
    north_list = lax.ppermute(list_message(forcing_pert[:, 0], cells[:128]), "lat", downward)

    surf, to_east, to_west, send_a, send_b = pick(
        forcing_pert, serve_cells, south_list, north_list, ocean_slots, remap_weight,
        ocean_seed, east_coef, north_coef, land_mask,
    )

    west = lax.ppermute(to_east, "lon", eastward)
    east = lax.ppermute(to_west, "lon", westward)
    send_a, send_b = corners(west, east, send_a, send_b)
    shift = ((fold_map[0] + 1) // COLS) % lon_count
    got_a = lax.ppermute(send_a, "lat", [(i ^ 1, i) for i in range(lat_count)])
    got_b = lax.switch(
        shift,
        [
            lambda v, s=s: lax.ppermute(v, ("lon", "lat"), ladder(lon_count, lat_count, s))
            for s in range(lon_count)
        ],
        send_b,
    )
    adjoint_two, total = steps(
        vert_coef, ocean_seed, surf, east_coef, north_coef, land_mask, to_east, to_west, west, east,
        send_a, send_b, got_a, got_b,
    )
    sums, to_north, to_south = spread(total, remap_weight, ocean_slots)
    from_south = lax.ppermute(to_north, "lat", upward)
    from_north = lax.ppermute(to_south, "lat", downward)
    stress_sens = gather(sums, from_south, from_north, serve_cells)
    return (adjoint_two, stress_sens)


def solution(mesh):
    return jax.shard_map(
        shards,
        mesh=mesh,
        in_specs=(
            P(None, None, "lat", "lon"),
            P(None, "lat", "lon"),
            P("lat", "lon"),
            P("lat", "lon"),
            P("lat", "lon"),
            P(),
            P(None, "lat", "lon"),
            P(None, "lat", "lon"),
            P("lat", "lon"),
            P(),
        ),
        out_specs=(P(None, None, "lat", "lon"), P(None, "lat", "lon")),
        check_vma=False,
    )
```

```python
import jax
import jax.numpy as jnp
from jax import lax
from jax.experimental import pallas as pl
from jax.experimental.pallas import tpu as pltpu
from jax.sharding import PartitionSpec as P

PL = 4
LEV = 10
ROWS = 128
COLS = 256
NPL = PL * LEV
MSG = 48
CORNER = 43
LISTS = 34
HI = 17
HPAD = 18
F32 = jnp.float32
BF16 = jnp.bfloat16
GROUPS = ROWS // 8
VM = pltpu.CompilerParams(vmem_limit_bytes=56 * 1024 * 1024)


def lane_iota(shape):
    return lax.broadcasted_iota(jnp.int32, shape, len(shape) - 1)


def row_iota(shape):
    return lax.broadcasted_iota(jnp.int32, shape, len(shape) - 2)


def lookup(row, low):
    table = jnp.broadcast_to(row, low.shape)
    return jnp.take_along_axis(table, low, axis=1, mode="promise_in_bounds")


def pick_body(
    forcing, serve, south, north, slots, weights, seed, east, north_c, land,
    surf, to_east, to_west, send_a, send_b, pool,
):
    even = lax.axis_index("lat") % 2 == 0
    step = pl.program_id(0)
    steps = pl.num_programs(0)

    @pl.when(step == 0)
    def _():
        pool[:, LISTS:, :] = jnp.zeros((PL, 40 - LISTS, 128), F32)
        for g in range(4):
            ids = jnp.concatenate(
                [serve[:, 128 * (8 * g + i + 1) : 128 * (8 * g + i + 2)] for i in range(8)], axis=0
            )
            low = ids & 127
            high = ids >> 7
            acc = [jnp.zeros((8, 128), F32) for _ in range(PL)]
            for h in range(32):
                hit = high == h
                for p in range(PL):
                    acc[p] = jnp.where(hit, lookup(forcing[p, h : h + 1, :], low), acc[p])
            for p in range(PL):
                pool[p, 1 + 8 * g : 9 + 8 * g, :] = acc[p]
        for recv, place in ((south, 0), (north, LISTS - 1)):
            low = jnp.broadcast_to(recv[4:5, :].astype(jnp.int32) & 127, (8, 128))
            for p in range(PL):
                got = lookup(recv[p : p + 1, :], low)
                pool[p, place : place + 1, :] = got[0:1, :]

    block = surf.shape[1]
    lanes = lane_iota((8, 128))
    for g in range(block // 8):
        rs = slice(8 * g, 8 * g + 8)
        image = []
        for t in range(2):
            cs = slice(128 * t, 128 * t + 128)
            acc = []
            for k in range(2):
                ids = slots[k, rs, cs]
                low = ids & 127
                high = ids >> 7
                own = [jnp.zeros((8, 128), F32) for _ in range(PL)]
                for h in range(LISTS):
                    hit = high == h
                    for p in range(PL):
                        own[p] = jnp.where(hit, lookup(pool[p, h : h + 1, :], low), own[p])
                acc.append(own)
            image.append(
                [weights[0, rs, cs] * acc[0][p] + weights[1, rs, cs] * acc[1][p] for p in range(PL)]
            )
        for p in range(PL):
            surf[p, rs, 0:128] = image[0][p]
            surf[p, rs, 128:256] = image[1][p]
        pair = lanes >> 1
        statics = (east, north_c, land)
        for t, out, first in ((0, to_west, 0), (1, to_east, 126)):
            cs = slice(128 * t, 128 * t + 128)
            acc = jnp.zeros((8, 128), F32)
            for m in range(NPL + 3):
                if m < NPL:
                    p, k = divmod(m, LEV)
                    v = seed[p, k, rs, cs]
                    if k == 0:
                        v = v + image[t][p]
                else:
                    v = statics[m - NPL][rs, cs].astype(F32)
                shift = (2 * m - first) % 128
                if shift:
                    v = pltpu.roll(v, shift, 1)
                acc = jnp.where(pair == m, v, acc)
            out[rs, :] = acc

    def rows_out(out, adjacent, second):
        out[...] = jnp.zeros_like(out)
        for c, r in ((0, adjacent), (1, second)):
            for t in range(2):
                cs = slice(128 * t, 128 * t + 128)
                for m in range(NPL):
                    p, k = divmod(m, LEV)
                    v = seed[p, k, r : r + 1, cs]
                    if k == 0:
                        v = v + surf[p, r : r + 1, cs]
                    out[2 * c + t, m : m + 1, :] = v
                out[2 * c + t, 40:41, :] = east[r : r + 1, cs]
                out[2 * c + t, 41:42, :] = north_c[r : r + 1, cs]
                out[2 * c + t, 42:43, :] = land[r : r + 1, cs].astype(F32)

    for flag, low_out, high_out in ((even, send_b, send_a), (jnp.logical_not(even), send_a, send_b)):

        @pl.when(jnp.logical_and(flag, step == 0))
        def _():
            rows_out(low_out, 0, 1)

        @pl.when(jnp.logical_and(flag, step == steps - 1))
        def _():
            rows_out(high_out, block - 1, block - 2)


def pick(forcing, serve, south, north, slots, weights, seed, east, north_c, land):
    block = 16
    whole = lambda *shape: pl.BlockSpec(shape, lambda i: (0,) * len(shape))
    tile = pl.BlockSpec((block, COLS), lambda i: (i, 0))
    pair = pl.BlockSpec((2, block, COLS), lambda i: (0, i, 0))
    return pl.pallas_call(
        pick_body,
        grid=(ROWS // block,),
        in_specs=[
            whole(PL, 32, 128), whole(1, LISTS * 128), whole(8, 128), whole(8, 128), pair, pair,
            pl.BlockSpec((PL, LEV, block, COLS), lambda i: (0, 0, i, 0)), tile, tile, tile,
        ],
        out_specs=[
            pl.BlockSpec((PL, block, COLS), lambda i: (0, i, 0)),
            pl.BlockSpec((block, 128), lambda i: (i, 0)),
            pl.BlockSpec((block, 128), lambda i: (i, 0)),
            whole(4, MSG, 128),
            whole(4, MSG, 128),
        ],
        out_shape=[
            jax.ShapeDtypeStruct((PL, ROWS, COLS), F32),
            jax.ShapeDtypeStruct((ROWS, 128), F32),
            jax.ShapeDtypeStruct((ROWS, 128), F32),
            jax.ShapeDtypeStruct((4, MSG, 128), F32),
            jax.ShapeDtypeStruct((4, MSG, 128), F32),
        ],
        scratch_shapes=[pltpu.VMEM((PL, 40, 128), F32)],
        compiler_params=VM,
        name="pick",
    )(forcing, serve, south, north, slots, weights, seed, east, north_c, land)


def corner_body(west_first, west_last, east_first, east_last, tile_a, tile_b, out_a, out_b):
    even = lax.axis_index("lat") % 2 == 0
    odd = (lane_iota((8, 128)) & 1) == 1
    low = jnp.where(odd, west_first[0:1, :], east_first[0:1, :])
    high = jnp.where(odd, west_last[7:8, :], east_last[7:8, :])
    here = row_iota((8, 128)) == CORNER - 40
    out_a[0] = jnp.where(here, jnp.where(even, high, low), tile_a[0])
    out_b[0] = jnp.where(here, jnp.where(even, low, high), tile_b[0])


def corners(west, east, send_a, send_b):
    first = pl.BlockSpec((8, 128), lambda i: (0, 0))
    last = pl.BlockSpec((8, 128), lambda i: (GROUPS - 1, 0))
    spot = pl.BlockSpec((1, 8, 128), lambda i: (0, 5, 0))
    message = jax.ShapeDtypeStruct((4, MSG, 128), F32)
    return pl.pallas_call(
        corner_body,
        grid=(1,),
        in_specs=[first, last, first, last, spot, spot],
        out_specs=[spot, spot],
        out_shape=[message, message],
        input_output_aliases={4: 0, 5: 1},
        name="corners",
    )(west, west, east, east, send_a, send_b)


def ring(
    vert, to_east, to_west, west, east, send_a, send_b, got_a, got_b,
    rows_south, rows_north, rows_south1, rows_north1, west1, east1,
):
    place = lax.axis_index("lat")
    even = place % 2 == 0
    fold = place == lax.axis_size("lat") - 1
    lanes = lane_iota((1, 128))
    odd = (lanes & 1) == 1

    def chosen(flag, yes, no):
        return jnp.where(flag, yes, no)

    a = got_a[...]
    b = got_b[...]
    above = chosen(even, a, b)
    below = chosen(even, b, a)
    top = chosen(even, send_a[...], send_b[...])
    bottom = chosen(even, send_b[...], send_a[...])
    back = 127 - lane_iota((MSG, 128))
    flip = lambda x: jnp.take_along_axis(x, back, axis=1, mode="promise_in_bounds")
    turned = [flip(above[1]), flip(above[0]), flip(above[3]), flip(above[2])]
    corner_above = above[0, CORNER : CORNER + 1, :]
    corner_below = below[0, CORNER : CORNER + 1, :]
    swapped = jnp.where(odd, pltpu.roll(corner_above, 1, 1), pltpu.roll(corner_above, 127, 1))
    pick_lane = lambda x, lane: jnp.sum(jnp.where(lane_iota(x.shape) == lane, x, 0.0), axis=1, keepdims=True)
    e_above = jnp.concatenate([above[0, 40:41, :], above[1, 40:41, :]], axis=1)
    e_turn = jnp.concatenate([turned[0][40:41, :], turned[1][40:41, :]], axis=1)
    wide = lane_iota((1, COLS))
    e_edge = pick_lane(corner_above, 81)
    e_fold = jnp.where(wide == 255, e_edge, pltpu.roll(e_turn, 255, 1))
    e_fold_west = e_turn[:, 0:1]

    n0 = jnp.concatenate([chosen(fold, turned[0], above[0]), chosen(fold, turned[1], above[1])], axis=1)
    n1 = jnp.concatenate([chosen(fold, turned[2], above[2]), chosen(fold, turned[3], above[3])], axis=1)
    s0 = jnp.concatenate([below[0], below[1]], axis=1)
    s1 = jnp.concatenate([below[2], below[3]], axis=1)
    own_top = jnp.concatenate([top[0], top[1]], axis=1)
    own_bottom = jnp.concatenate([bottom[0], bottom[1]], axis=1)
    corner_n = chosen(fold, swapped, corner_above)
    e_n = chosen(fold, e_fold, e_above)
    e_n_west = chosen(fold, e_fold_west, e_edge)
    toward_n = chosen(fold, n0[41:42, :], own_top[41:42, :])
    away_n = chosen(fold, n1[41:42, :], n0[41:42, :])

    def level_coefs(plane):
        level = plane % LEV
        upper = jnp.zeros(plane.shape, F32)
        lower = jnp.zeros(plane.shape, F32)
        for k in range(LEV - 1):
            upper = jnp.where(level == k, vert[k], upper)
            lower = jnp.where(level == k + 1, vert[k], lower)
        return upper, lower

    row_up, row_down = level_coefs(row_iota((MSG, COLS)))

    def row_step(cur, toward, away, toward_c, away_c, e_row, e_west, corner):
        spread = jnp.broadcast_to(corner, (MSG, 128))
        where = lane_iota((MSG, 128))
        plane = row_iota((MSG, 128))
        from_west = jnp.sum(jnp.where(where == 2 * plane + 1, spread, 0.0), axis=1, keepdims=True)
        from_east = jnp.sum(jnp.where(where == 2 * plane, spread, 0.0), axis=1, keepdims=True)
        lane = lane_iota((MSG, COLS))
        east_u = jnp.where(lane == COLS - 1, from_east, pltpu.roll(cur, COLS - 1, 1))
        west_u = jnp.where(lane == 0, from_west, pltpu.roll(cur, 1, 1))
        e_left = jnp.where(wide == 0, e_west, pltpu.roll(e_row, 1, 1))
        up = pltpu.roll(cur, MSG - 1, 0)
        down = pltpu.roll(cur, 1, 0)
        wet = cur[42:43, :]
        return wet * (
            cur
            + e_row * (east_u - cur)
            + e_left * (west_u - cur)
            + toward_c * (toward - cur)
            + away_c * (away - cur)
            + row_up * (up - cur)
            + row_down * (down - cur)
        )

    n_first = row_step(n0, own_top, n1, toward_n, away_n, e_n, e_n_west, corner_n)
    s_first = row_step(
        s0, own_bottom, s1, s0[41:42, :], s1[41:42, :], s0[40:41, :], pick_lane(corner_below, 81), corner_below
    )
    rows_north[...] = n0
    rows_south[...] = s0
    rows_north1[...] = n_first
    rows_south1[...] = s_first

    shape = (ROWS, 128)
    lane = lane_iota(shape)
    row = row_iota(shape)
    col_up, col_down = level_coefs(lane_iota((1, 128)) >> 1)

    def col_step(cur, east_u, west_u, e_right, e_left, n_col, n_south, wet):
        north_u = jnp.where(row == ROWS - 1, corner_n, pltpu.roll(cur, ROWS - 1, 0))
        south_u = jnp.where(row == 0, corner_below, pltpu.roll(cur, 1, 0))
        n_below = jnp.where(row_iota((ROWS, 1)) == 0, n_south, pltpu.roll(jnp.broadcast_to(n_col, shape), 1, 0))
        return wet * (
            cur
            + e_right * (east_u - cur)
            + e_left * (west_u - cur)
            + n_col * (north_u - cur)
            + n_below * (south_u - cur)
            + col_up * (pltpu.roll(cur, 126, 1) - cur)
            + col_down * (pltpu.roll(cur, 2, 1) - cur)
        )

    w = west[...]
    e = east[...]
    mine_w = to_west[...]
    mine_e = to_east[...]
    lane_of = lambda x, n: x[:, n : n + 1]
    west1[...] = col_step(
        w, pltpu.roll(mine_w, 1, 1), pltpu.roll(w, 1, 1), lane_of(w, 81), lane_of(w, 80),
        lane_of(w, 83), pick_lane(corner_below, 83), lane_of(w, 85),
    )
    east1[...] = col_step(
        e, pltpu.roll(e, 127, 1), pltpu.roll(mine_e, 127, 1), lane_of(e, 80), lane_of(mine_e, 81),
        lane_of(e, 82), pick_lane(corner_below, 82), lane_of(e, 84),
    )


def hot_low(ids):
    grid = row_iota((COLS, ids.shape[1]))
    return jnp.where(grid == (ids & 255), 1.0, 0.0).astype(BF16)


def hot_high(ids, parts, count):
    high = jnp.broadcast_to(ids >> 8, parts.shape)
    return jnp.concatenate([jnp.where(high == h, parts, 0.0) for h in range(count)], axis=0).astype(BF16)


def two_parts(values):
    big = values.astype(BF16).astype(F32)
    return jnp.concatenate([big, values - big], axis=0)


CONTRACT = (((1,), (1,)), ((), ()))


def sweep_body(
    vert, seed, surf, east, north, land, to_east, to_west, west0, east0, send_a, send_b, got_a, got_b,
    weights, slots,
    out, sums, to_north, to_south,
    start0, start1, start2, start3, first0, first1, first2, first3, result, total, coef, side,
    west1, east1, south0, north0, south1, north1, grid_low, arrive, leave,
):
    start = (start0, start1, start2, start3)
    first = (first0, first1, first2, first3)

    def incoming(p, g):
        row = pl.multiple_of(g * 8, 8)
        return pltpu.make_async_copy(
            seed.at[p, :, pl.ds(row, 8), :], start[p].at[:, pl.ds(row + 8, 8), :], arrive.at[p, g]
        )

    def outgoing(g):
        rows = pl.ds(pl.multiple_of(g * 8, 8), 8)
        return pltpu.make_async_copy(result.at[:, :, rows, :], out.at[:, :, rows, :], leave.at[g])

    def fetch(g, carry):
        for p in range(PL):
            incoming(p, g).start()
        return carry

    lax.fori_loop(0, GROUPS, fetch, 0)

    ring(
        vert, to_east, to_west, west0, east0, send_a, send_b, got_a, got_b,
        south0, north0, south1, north1, west1, east1,
    )
    wide = lane_iota((ROWS, COLS))
    tall = row_iota((ROWS, COLS))
    e = east[...]
    n = north[...]
    wet = land[...].astype(F32)
    e_left = jnp.where(wide == 0, west0[:, 81:82], pltpu.roll(e, 1, 1))
    n_below = jnp.where(tall == 0, south0[41:42, :], pltpu.roll(n, 1, 0))
    coef[0] = wet * e
    coef[1] = wet * e_left
    coef[2] = wet * n
    coef[3] = wet * n_below
    coef[4] = wet - wet * (e + e_left + n + n_below)
    coef[5] = wet
    odd = (lane_iota((ROWS, 128)) & 1) == 1
    for i, w, x in ((0, west0, east0), (1, west1, east1)):
        pack = jnp.where(odd, w[...], pltpu.roll(x[...], 2, 1))
        for p in range(PL):
            for k in range(LEV):
                side[i, p, k] = pltpu.roll(pack, (126 - 2 * k - 2 * LEV * p) % 128, 1)
    for p in range(PL):
        for k in range(LEV):
            m = p * LEV + k
            start[p][k, 7:8, :] = south0[m : m + 1, :]
            start[p][k, 136:137, :] = north0[m : m + 1, :]
            first[p][k, 7:8, :] = south1[m : m + 1, :]
            first[p][k, 136:137, :] = north1[m : m + 1, :]
    grid_low[...] = row_iota((COLS, COLS)).astype(F32).astype(BF16)
    which = (row_iota((16, COLS)) >> 3).astype(F32)
    lane = lane_iota((8, 128))
    sub = row_iota((8, 128))
    cs = (slice(0, 128), slice(128, 256))

    def ready(g):
        row = pl.multiple_of(g * 8, 8)
        for p in range(PL):
            incoming(p, g).wait()
        for p in range(PL):
            here = pl.ds(row + 8, 8)
            start[p][0, here, :] = start[p][0, here, :] + surf[p, pl.ds(row, 8), :]

    def stencil(p, g, src, at, c, store):
        row = pl.multiple_of(g * 8, 8)
        here = pl.ds(row + 8, 8)
        below = [None, None]
        u = [src[0, here, cs[t]] for t in range(2)]
        for k in range(LEV):
            edge = side[at, p, k, pl.ds(row, 8), :]
            east_of = [jnp.where(lane == 0, u[1], u[0]), jnp.where(lane == 0, edge, u[1])]
            west_of = [jnp.where(lane == 127, edge, u[0]), jnp.where(lane == 127, u[0], u[1])]
            ahead = [None, None]
            for t in range(2):
                up_rows = src[k, pl.ds(row + 16, 8), cs[t]]
                dn_rows = src[k, pl.ds(row, 8), cs[t]]
                north_u = pltpu.roll(jnp.where(sub == 0, up_rows, u[t]), 7, 0)
                south_u = pltpu.roll(jnp.where(sub == 7, dn_rows, u[t]), 1, 0)
                east_u = pltpu.roll(east_of[t], 127, 1)
                west_u = pltpu.roll(west_of[t], 1, 1)
                new = (
                    c[4][t] * u[t]
                    + c[0][t] * east_u
                    + c[1][t] * west_u
                    + c[2][t] * north_u
                    + c[3][t] * south_u
                )
                flux = None
                if k + 1 < LEV:
                    ahead[t] = src[k + 1, here, cs[t]]
                    flux = vert[k] * (ahead[t] - u[t])
                if flux is None:
                    new = new - c[5][t] * below[t]
                elif below[t] is None:
                    new = new + c[5][t] * flux
                else:
                    new = new + c[5][t] * (flux - below[t])
                below[t] = flux
                store(k, row, t, new)
            u = ahead

    def coefs(g):
        row = pl.multiple_of(g * 8, 8)
        return [[coef[i, pl.ds(row, 8), cs[t]] for t in range(2)] for i in range(6)]

    def step_one(p, g, c):
        def keep(k, row, t, new):
            first[p][k, pl.ds(row + 8, 8), cs[t]] = new

        stencil(p, g, start[p], 0, c, keep)

    def step_two(p, g, c):
        def finish(k, row, t, new):
            result[p, k, pl.ds(row, 8), cs[t]] = new
            if k == 0:
                total[p, pl.ds(row, 8), cs[t]] = new + first[p][0, pl.ds(row + 8, 8), cs[t]]

        stencil(p, g, first[p], 1, c, finish)

    def surfaces(g):
        rows = pl.ds(pl.multiple_of(g * 8, 8), 8)
        return (
            [slots[k, rows, :] for k in range(2)],
            [weights[k, rows, :] for k in range(2)],
            [total[p, rows, :] for p in range(PL)],
        )

    def slot_sums(accs, loaded, lines):
        ids_all, w_all, t_all = loaded
        for r in lines:
            surface = jnp.concatenate([t[r : r + 1, :] for t in t_all], axis=0)
            for k in range(2):
                ids = ids_all[k][r : r + 1, :]
                low = jnp.broadcast_to((ids & 255).astype(F32), (16, COLS)).astype(BF16)
                low = jnp.concatenate([low] * 16, axis=0)
                one_hot = jnp.where(grid_low[...] == low, jnp.array(1, BF16), jnp.array(0, BF16))
                parts = two_parts(surface * w_all[k][r : r + 1, :])
                parts = jnp.concatenate([parts, parts], axis=0).astype(BF16)
                high = (jnp.broadcast_to((ids >> 8).astype(F32), (16, COLS)) - which).astype(BF16)
                hot = jnp.concatenate(
                    [
                        jnp.where(high == jnp.array(2 * h, BF16), parts, jnp.array(0, BF16))
                        for h in range(HPAD // 2)
                    ],
                    axis=0,
                )
                pltpu.matmul_push_rhs(one_hot, r % 2, k, transpose=True)
                pltpu.matmul_acc_lhs(accs[k], hot, load_staged_rhs=r % 2)

    def accumulate(*accs):
        ready(0)
        ready(1)

        def lead(g, carry):
            c = coefs(g)
            ready(g + 2)
            for p in range(PL):
                step_one(p, g, c)
            return carry

        lax.fori_loop(0, 2, lead, 0)
        ready(4)
        c = coefs(0)
        for p in range(PL):
            step_two(p, 0, c)
        c = coefs(2)
        for p in range(PL):
            step_one(p, 2, c)
        outgoing(0).start()

        def body(i, carry):
            @pl.when(i < GROUPS - 2)
            def _():
                ready(i + 2)

            loaded = surfaces(i - 3)
            c_two = coefs(i - 2)
            c_one = coefs(i)
            for p in range(PL):
                slot_sums(accs, loaded, (2 * p, 2 * p + 1))
                step_two(p, i - 2, c_two)
                step_one(p, i, c_one)
            outgoing(i - 2).start()
            return carry

        lax.fori_loop(3, GROUPS, body, 0)

        def trail(g, carry):
            loaded = surfaces(g - 1)
            c = coefs(g)
            for p in range(PL):
                slot_sums(accs, loaded, (2 * p, 2 * p + 1))
                step_two(p, g, c)
            outgoing(g).start()
            return carry

        lax.fori_loop(GROUPS - 2, GROUPS, trail, 0)
        slot_sums(accs, surfaces(GROUPS - 1), range(8))
        summed = pltpu.matmul_pop(accs[0]) + pltpu.matmul_pop(accs[1])
        sums[...] = summed
        to_north[...] = summed[128:136, 128:] + pltpu.roll(summed[128:136, 128:], 4, 0)
        to_south[...] = summed[0:8, :128] + pltpu.roll(summed[0:8, :128], 4, 0)

    pl.run_scoped(accumulate, *[pltpu.ACC(m)((HPAD * 8, COLS), F32) for m in range(2)])

    def drain(g, carry):
        outgoing(g).wait()
        return carry

    lax.fori_loop(0, GROUPS, drain, 0)


def sweep(vert, seed, surf, east, north, land, to_east, to_west, west, east_in, send_a, send_b, got_a, got_b,
          weights, slots):
    whole = lambda *shape: pl.BlockSpec(shape, lambda i: (0,) * len(shape))
    tile = whole(ROWS, COLS)
    cols = whole(ROWS, 128)
    message = whole(4, MSG, 128)
    pair = whole(2, ROWS, COLS)
    anywhere = pl.BlockSpec(memory_space=pl.ANY)
    small = jax.ShapeDtypeStruct((8, 128), F32)
    padded = pltpu.VMEM((LEV, ROWS + 16, COLS), F32)
    return pl.pallas_call(
        sweep_body,
        grid=(1,),
        in_specs=[pl.BlockSpec(memory_space=pltpu.SMEM), anywhere, whole(PL, ROWS, COLS), tile, tile, tile]
        + [cols] * 4
        + [message] * 4
        + [pair] * 2,
        out_specs=[anywhere, whole(HPAD * 8, COLS), whole(8, 128), whole(8, 128)],
        out_shape=[
            jax.ShapeDtypeStruct((PL, LEV, ROWS, COLS), F32),
            jax.ShapeDtypeStruct((HPAD * 8, COLS), F32),
            small,
            small,
        ],
        scratch_shapes=[padded] * 8
        + [
            pltpu.VMEM((PL, LEV, ROWS, COLS), F32),
            pltpu.VMEM((PL, ROWS, COLS), F32),
            pltpu.VMEM((6, ROWS, COLS), F32),
            pltpu.VMEM((2, PL, LEV, ROWS, 128), F32),
            pltpu.VMEM((ROWS, 128), F32),
            pltpu.VMEM((ROWS, 128), F32),
        ]
        + [pltpu.VMEM((MSG, COLS), F32)] * 4
        + [
            pltpu.VMEM((COLS, COLS), BF16),
            pltpu.SemaphoreType.DMA((PL, GROUPS)),
            pltpu.SemaphoreType.DMA((GROUPS,)),
        ],
        compiler_params=VM,
        name="sweep",
    )(vert, seed, surf, east, north, land, to_east, to_west, west, east_in, send_a, send_b, got_a, got_b,
      weights, slots)


def gather_body(sums, south, north, serve, out):
    lane = lane_iota((PL, COLS))
    acc = jnp.zeros((128, COLS), F32)
    for h in range(HI):
        tile = sums[8 * h : 8 * h + 8, :]
        values = tile[0:4, :] + tile[4:8, :]
        if h == 0:
            values = jnp.where(lane < 128, jnp.concatenate([south[0:4, :], south[0:4, :]], axis=1), values)
        if h == HI - 1:
            values = jnp.where(lane >= 128, jnp.concatenate([north[0:4, :], north[0:4, :]], axis=1), values)
        ids = serve[:, COLS * h : COLS * h + COLS]
        acc = acc + lax.dot_general(
            hot_high(ids, two_parts(values), 16), hot_low(ids), CONTRACT, preferred_element_type=F32
        )
    for h in range(16):
        tile = acc[8 * h : 8 * h + 8, :]
        values = tile[0:4, :] + tile[4:8, :]
        for p in range(PL):
            for t in range(2):
                out[p, 2 * h + t : 2 * h + t + 1, :] = values[p : p + 1, 128 * t : 128 * t + 128]


def gather(sums, south, north, serve):
    whole = lambda *shape: pl.BlockSpec(shape, lambda i: (0,) * len(shape))
    return pl.pallas_call(
        gather_body,
        grid=(1,),
        in_specs=[whole(HPAD * 8, COLS), whole(8, 128), whole(8, 128), whole(1, LISTS * 128)],
        out_specs=whole(PL, 32, 128),
        out_shape=jax.ShapeDtypeStruct((PL, 32, 128), F32),
        compiler_params=VM,
        name="gather",
    )(sums, south, north, serve)


def ladder(lon_count, lat_count, shift):
    place = lambda a, j: j * lat_count + a
    pairs = []
    for j in range(lon_count):
        for a in range(1, lat_count - 1, 2):
            pairs.append((place(a, j), place(a + 1, j)))
            pairs.append((place(a + 1, j), place(a, j)))
        pairs.append((place(lat_count - 1, j), place(lat_count - 1, (shift - 1 - j) % lon_count)))
    return pairs


def shards(
    ocean_seed, forcing_pert, land_mask, east_coef, north_coef, vert_coef, remap_weight, ocean_slots,
    serve_cells, fold_map,
):
    lat_count = lax.axis_size("lat")
    lon_count = lax.axis_size("lon")
    upward = [(i, i + 1) for i in range(lat_count - 1)]
    downward = [(i + 1, i) for i in range(lat_count - 1)]
    eastward = [(i, (i + 1) % lon_count) for i in range(lon_count)]
    westward = [((i + 1) % lon_count, i) for i in range(lon_count)]

    cells = serve_cells.reshape(-1)

    def list_message(row, ids):
        return jnp.concatenate([row, ids.astype(F32)[None], jnp.zeros((3, 128), F32)], axis=0)

    south_list = lax.ppermute(list_message(forcing_pert[:, -1], cells[-128:]), "lat", upward)
    north_list = lax.ppermute(list_message(forcing_pert[:, 0], cells[:128]), "lat", downward)

    shift = ((fold_map[0] + 1) // COLS) % lon_count
    shift, forcing = lax.optimization_barrier((shift, forcing_pert))

    surf, to_east, to_west, send_a, send_b = pick(
        forcing, serve_cells, south_list, north_list, ocean_slots, remap_weight,
        ocean_seed, east_coef, north_coef, land_mask,
    )

    west = lax.ppermute(to_east, "lon", eastward)
    east = lax.ppermute(to_west, "lon", westward)
    send_a, send_b = corners(west, east, send_a, send_b)
    got_a = lax.ppermute(send_a, "lat", [(i ^ 1, i) for i in range(lat_count)])
    got_b = lax.switch(
        shift,
        [
            lambda v, s=s: lax.ppermute(v, ("lon", "lat"), ladder(lon_count, lat_count, s))
            for s in range(lon_count)
        ],
        send_b,
    )
    adjoint_two, sums, to_north, to_south = sweep(
        vert_coef, ocean_seed, surf, east_coef, north_coef, land_mask, to_east, to_west, west, east,
        send_a, send_b, got_a, got_b, remap_weight, ocean_slots,
    )
    from_south = lax.ppermute(to_north, "lat", upward)
    from_north = lax.ppermute(to_south, "lat", downward)
    stress_sens = gather(sums, from_south, from_north, serve_cells)
    return (adjoint_two, stress_sens)


def solution(mesh):
    return jax.shard_map(
        shards,
        mesh=mesh,
        in_specs=(
            P(None, None, "lat", "lon"),
            P(None, "lat", "lon"),
            P("lat", "lon"),
            P("lat", "lon"),
            P("lat", "lon"),
            P(),
            P(None, "lat", "lon"),
            P(None, "lat", "lon"),
            P("lat", "lon"),
            P(),
        ),
        out_specs=(P(None, None, "lat", "lon"), P(None, "lat", "lon")),
        check_vma=False,
    )
```

```python
import jax
import jax.numpy as jnp
from jax import lax
from jax.experimental import pallas as pl
from jax.experimental.pallas import tpu as pltpu
from jax.sharding import PartitionSpec as P

PL = 4
LEV = 10
ROWS = 128
COLS = 256
NPL = PL * LEV
MSG = 48
CORNER = 43
LISTS = 34
HI = 17
HPAD = 18
F32 = jnp.float32
BF16 = jnp.bfloat16
GROUPS = ROWS // 8
VM = pltpu.CompilerParams(vmem_limit_bytes=64 * 1024 * 1024)


def lane_iota(shape):
    return lax.broadcasted_iota(jnp.int32, shape, len(shape) - 1)


def row_iota(shape):
    return lax.broadcasted_iota(jnp.int32, shape, len(shape) - 2)


def lookup(row, low):
    table = jnp.broadcast_to(row, low.shape)
    return jnp.take_along_axis(table, low, axis=1, mode="promise_in_bounds")


BLOCK = 16


def pick_body(
    forcing, serve, south, north, slots, weights, seed_hbm, east, north_c, land,
    surf, to_east, to_west, send_a, send_b,
    seed, pool, table, halves, grid_low, left, right, arrive,
):
    even = lax.axis_index("lat") % 2 == 0

    def incoming(i):
        rows = pl.ds(pl.multiple_of(i * BLOCK, BLOCK), BLOCK)
        return pltpu.make_async_copy(seed_hbm.at[:, :, rows, :], seed.at[:, :, rows, :], arrive.at[i])

    def fetch(i, carry):
        incoming(i).start()
        return carry

    lax.fori_loop(0, ROWS // BLOCK, fetch, 0)

    pool[:, LISTS:, :] = jnp.zeros((PL, 40 - LISTS, 128), F32)
    for g in range(4):
        ids = jnp.concatenate(
            [serve[:, 128 * (8 * g + i + 1) : 128 * (8 * g + i + 2)] for i in range(8)], axis=0
        )
        low = ids & 127
        high = ids >> 7
        acc = [jnp.zeros((8, 128), F32) for _ in range(PL)]
        for h in range(32):
            hit = high == h
            for p in range(PL):
                acc[p] = jnp.where(hit, lookup(forcing[p, h : h + 1, :], low), acc[p])
        for p in range(PL):
            pool[p, 1 + 8 * g : 9 + 8 * g, :] = acc[p]
    for recv, place in ((south, 0), (north, LISTS - 1)):
        low = jnp.broadcast_to(recv[4:5, :].astype(jnp.int32) & 127, (8, 128))
        for p in range(PL):
            got = lookup(recv[p : p + 1, :], low)
            pool[p, place : place + 1, :] = got[0:1, :]
    for h in range(HPAD):
        for t in range(2):
            rows = jnp.concatenate([pool[p, 2 * h + t : 2 * h + t + 1, :] for p in range(PL)], axis=0)
            halves[8 * h : 8 * h + 8, 128 * t : 128 * t + 128] = two_parts(rows)
    table[...] = halves[...].astype(BF16)
    grid_low[...] = row_iota((COLS, COLS)).astype(F32).astype(BF16)

    lanes = lane_iota((8, 128))
    pair = lanes >> 1
    tiles = (slice(0, 128), slice(128, 256))
    statics = (east, north_c, land)

    def images(*accs):
        def body(i, carry):
            incoming(i).wait()
            groups = [pl.ds(pl.multiple_of(i * BLOCK + 8 * g, 8), 8) for g in range(BLOCK // 8)]
            ids_one = [slots[1, rs, :] for rs in groups]
            w_one = [weights[1, rs, :] for rs in groups]

            def issue(r):
                ids = ids_one[r // 8][r % 8 : r % 8 + 1, :]
                low = jnp.broadcast_to((ids & 255).astype(F32), (16, COLS)).astype(BF16)
                low = jnp.concatenate([low] * 16, axis=0)
                one_hot = jnp.where(grid_low[...] == low, jnp.array(1, BF16), jnp.array(0, BF16))
                pltpu.matmul_push_rhs(one_hot, (r // 2) % 2, r % 2)
                pltpu.matmul_acc_lhs(accs[r % 4], table[...], load_staged_rhs=(r // 2) % 2)

            def collect(r):
                got = pltpu.matmul_pop(accs[r % 4])
                high = jnp.broadcast_to(ids_one[r // 8][r % 8 : r % 8 + 1, :] >> 8, (8, COLS))
                mine = jnp.zeros((8, COLS), F32)
                for h in range(HI):
                    mine = jnp.where(high == h, got[8 * h : 8 * h + 8, :], mine)
                mine = (mine + pltpu.roll(mine, 4, 0)) * w_one[r // 8][r % 8 : r % 8 + 1, :]
                left[8 * r : 8 * r + 8, :] = mine[:, :128]
                right[8 * r : 8 * r + 8, :] = mine[:, 128:]

            zero = []
            for unit in range(BLOCK // 4):
                g, t = divmod(unit, 2)
                ids = slots[0, groups[g], tiles[t]]
                low = ids & 127
                high = ids >> 7
                own = [jnp.zeros((8, 128), F32) for _ in range(PL)]
                for h in range(LISTS):
                    if h % 8 == 0 and h < 32:
                        r = 4 * unit + h // 8
                        issue(r)
                        if r >= 2:
                            collect(r - 2)
                    hit = high == h
                    for p in range(PL):
                        own[p] = jnp.where(hit, lookup(pool[p, h : h + 1, :], low), own[p])
                zero.append([weights[0, groups[g], tiles[t]] * own[p] for p in range(PL)])
            collect(BLOCK - 2)
            collect(BLOCK - 1)

            for g, rs in enumerate(groups):
                for t, part, out, first in ((0, left, to_west, 0), (1, right, to_east, 126)):
                    image = []
                    for p in range(PL):
                        image.append(zero[2 * g + t][p] + part[pl.ds(64 * g + p, 8, stride=8), :])
                        surf[p, rs, tiles[t]] = image[p]
                    acc = jnp.zeros((8, 128), F32)
                    for m in range(NPL + 3):
                        if m < NPL:
                            p, k = divmod(m, LEV)
                            v = seed[p, k, rs, tiles[t]]
                            if k == 0:
                                v = v + image[p]
                        else:
                            v = statics[m - NPL][rs, tiles[t]].astype(F32)
                        shift = (2 * m - first) % 128
                        if shift:
                            v = pltpu.roll(v, shift, 1)
                        acc = jnp.where(pair == m, v, acc)
                    out[rs, :] = acc
            return carry

        lax.fori_loop(0, ROWS // BLOCK, body, 0)

    pl.run_scoped(images, *[pltpu.ACC(m % 2)((HPAD * 8, COLS), F32) for m in range(4)])

    def rows_out(out, adjacent, second):
        out[...] = jnp.zeros_like(out)
        for c, r in ((0, adjacent), (1, second)):
            for t in range(2):
                for m in range(NPL):
                    p, k = divmod(m, LEV)
                    v = seed[p, k, r : r + 1, tiles[t]]
                    if k == 0:
                        v = v + surf[p, r : r + 1, tiles[t]]
                    out[2 * c + t, m : m + 1, :] = v
                out[2 * c + t, 40:41, :] = east[r : r + 1, tiles[t]]
                out[2 * c + t, 41:42, :] = north_c[r : r + 1, tiles[t]]
                out[2 * c + t, 42:43, :] = land[r : r + 1, tiles[t]].astype(F32)

    for flag, low_out, high_out in ((even, send_b, send_a), (jnp.logical_not(even), send_a, send_b)):

        @pl.when(flag)
        def _():
            rows_out(low_out, 0, 1)
            rows_out(high_out, ROWS - 1, ROWS - 2)


def pick(forcing, serve, south, north, slots, weights, seed, east, north_c, land):
    whole = lambda *shape: pl.BlockSpec(shape, lambda i: (0,) * len(shape))
    tile = whole(ROWS, COLS)
    pair = whole(2, ROWS, COLS)
    shapes = [(PL, ROWS, COLS), (ROWS, 128), (ROWS, 128), (4, MSG, 128), (4, MSG, 128)]
    return pl.pallas_call(
        pick_body,
        grid=(1,),
        in_specs=[
            whole(PL, 32, 128), whole(1, LISTS * 128), whole(8, 128), whole(8, 128), pair, pair,
            pl.BlockSpec(memory_space=pl.ANY), tile, tile, tile,
        ],
        out_specs=[whole(*shape) for shape in shapes],
        out_shape=[jax.ShapeDtypeStruct(shape, F32) for shape in shapes],
        scratch_shapes=[
            pltpu.VMEM((PL, LEV, ROWS, COLS), F32),
            pltpu.VMEM((PL, 40, 128), F32),
            pltpu.VMEM((HPAD * 8, COLS), BF16),
            pltpu.VMEM((HPAD * 8, COLS), F32),
            pltpu.VMEM((COLS, COLS), BF16),
            pltpu.VMEM((8 * BLOCK, 128), F32),
            pltpu.VMEM((8 * BLOCK, 128), F32),
            pltpu.SemaphoreType.DMA((ROWS // BLOCK,)),
        ],
        compiler_params=VM,
        name="pick",
    )(forcing, serve, south, north, slots, weights, seed, east, north_c, land)


def corner_body(west_first, west_last, east_first, east_last, tile_a, tile_b, out_a, out_b):
    even = lax.axis_index("lat") % 2 == 0
    odd = (lane_iota((8, 128)) & 1) == 1
    low = jnp.where(odd, west_first[0:1, :], east_first[0:1, :])
    high = jnp.where(odd, west_last[7:8, :], east_last[7:8, :])
    here = row_iota((8, 128)) == CORNER - 40
    out_a[0] = jnp.where(here, jnp.where(even, high, low), tile_a[0])
    out_b[0] = jnp.where(here, jnp.where(even, low, high), tile_b[0])


def corners(west, east, send_a, send_b):
    first = pl.BlockSpec((8, 128), lambda i: (0, 0))
    last = pl.BlockSpec((8, 128), lambda i: (GROUPS - 1, 0))
    spot = pl.BlockSpec((1, 8, 128), lambda i: (0, 5, 0))
    message = jax.ShapeDtypeStruct((4, MSG, 128), F32)
    return pl.pallas_call(
        corner_body,
        grid=(1,),
        in_specs=[first, last, first, last, spot, spot],
        out_specs=[spot, spot],
        out_shape=[message, message],
        input_output_aliases={4: 0, 5: 1},
        name="corners",
    )(west, west, east, east, send_a, send_b)


def ring(
    vert, to_east, to_west, west, east, send_a, send_b, got_a, got_b,
    rows_south, rows_north, rows_south1, rows_north1, west1, east1,
):
    place = lax.axis_index("lat")
    even = place % 2 == 0
    fold = place == lax.axis_size("lat") - 1
    lanes = lane_iota((1, 128))
    odd = (lanes & 1) == 1

    def chosen(flag, yes, no):
        return jnp.where(flag, yes, no)

    a = got_a[...]
    b = got_b[...]
    above = chosen(even, a, b)
    below = chosen(even, b, a)
    top = chosen(even, send_a[...], send_b[...])
    bottom = chosen(even, send_b[...], send_a[...])
    back = 127 - lane_iota((MSG, 128))
    flip = lambda x: jnp.take_along_axis(x, back, axis=1, mode="promise_in_bounds")
    turned = [flip(above[1]), flip(above[0]), flip(above[3]), flip(above[2])]
    corner_above = above[0, CORNER : CORNER + 1, :]
    corner_below = below[0, CORNER : CORNER + 1, :]
    swapped = jnp.where(odd, pltpu.roll(corner_above, 1, 1), pltpu.roll(corner_above, 127, 1))
    pick_lane = lambda x, lane: jnp.sum(jnp.where(lane_iota(x.shape) == lane, x, 0.0), axis=1, keepdims=True)
    e_above = jnp.concatenate([above[0, 40:41, :], above[1, 40:41, :]], axis=1)
    e_turn = jnp.concatenate([turned[0][40:41, :], turned[1][40:41, :]], axis=1)
    wide = lane_iota((1, COLS))
    e_edge = pick_lane(corner_above, 81)
    e_fold = jnp.where(wide == 255, e_edge, pltpu.roll(e_turn, 255, 1))
    e_fold_west = e_turn[:, 0:1]

    n0 = jnp.concatenate([chosen(fold, turned[0], above[0]), chosen(fold, turned[1], above[1])], axis=1)
    n1 = jnp.concatenate([chosen(fold, turned[2], above[2]), chosen(fold, turned[3], above[3])], axis=1)
    s0 = jnp.concatenate([below[0], below[1]], axis=1)
    s1 = jnp.concatenate([below[2], below[3]], axis=1)
    own_top = jnp.concatenate([top[0], top[1]], axis=1)
    own_bottom = jnp.concatenate([bottom[0], bottom[1]], axis=1)
    corner_n = chosen(fold, swapped, corner_above)
    e_n = chosen(fold, e_fold, e_above)
    e_n_west = chosen(fold, e_fold_west, e_edge)
    toward_n = chosen(fold, n0[41:42, :], own_top[41:42, :])
    away_n = chosen(fold, n1[41:42, :], n0[41:42, :])

    def level_coefs(plane):
        level = plane % LEV
        upper = jnp.zeros(plane.shape, F32)
        lower = jnp.zeros(plane.shape, F32)
        for k in range(LEV - 1):
            upper = jnp.where(level == k, vert[k], upper)
            lower = jnp.where(level == k + 1, vert[k], lower)
        return upper, lower

    row_up, row_down = level_coefs(row_iota((MSG, COLS)))

    def row_step(cur, toward, away, toward_c, away_c, e_row, e_west, corner):
        spread = jnp.broadcast_to(corner, (MSG, 128))
        where = lane_iota((MSG, 128))
        plane = row_iota((MSG, 128))
        from_west = jnp.sum(jnp.where(where == 2 * plane + 1, spread, 0.0), axis=1, keepdims=True)
        from_east = jnp.sum(jnp.where(where == 2 * plane, spread, 0.0), axis=1, keepdims=True)
        lane = lane_iota((MSG, COLS))
        east_u = jnp.where(lane == COLS - 1, from_east, pltpu.roll(cur, COLS - 1, 1))
        west_u = jnp.where(lane == 0, from_west, pltpu.roll(cur, 1, 1))
        e_left = jnp.where(wide == 0, e_west, pltpu.roll(e_row, 1, 1))
        up = pltpu.roll(cur, MSG - 1, 0)
        down = pltpu.roll(cur, 1, 0)
        wet = cur[42:43, :]
        return wet * (
            cur
            + e_row * (east_u - cur)
            + e_left * (west_u - cur)
            + toward_c * (toward - cur)
            + away_c * (away - cur)
            + row_up * (up - cur)
            + row_down * (down - cur)
        )

    n_first = row_step(n0, own_top, n1, toward_n, away_n, e_n, e_n_west, corner_n)
    s_first = row_step(
        s0, own_bottom, s1, s0[41:42, :], s1[41:42, :], s0[40:41, :], pick_lane(corner_below, 81), corner_below
    )
    rows_north[...] = n0
    rows_south[...] = s0
    rows_north1[...] = n_first
    rows_south1[...] = s_first

    shape = (ROWS, 128)
    lane = lane_iota(shape)
    row = row_iota(shape)
    col_up, col_down = level_coefs(lane_iota((1, 128)) >> 1)

    def col_step(cur, east_u, west_u, e_right, e_left, n_col, n_south, wet):
        north_u = jnp.where(row == ROWS - 1, corner_n, pltpu.roll(cur, ROWS - 1, 0))
        south_u = jnp.where(row == 0, corner_below, pltpu.roll(cur, 1, 0))
        n_below = jnp.where(row_iota((ROWS, 1)) == 0, n_south, pltpu.roll(jnp.broadcast_to(n_col, shape), 1, 0))
        return wet * (
            cur
            + e_right * (east_u - cur)
            + e_left * (west_u - cur)
            + n_col * (north_u - cur)
            + n_below * (south_u - cur)
            + col_up * (pltpu.roll(cur, 126, 1) - cur)
            + col_down * (pltpu.roll(cur, 2, 1) - cur)
        )

    w = west[...]
    e = east[...]
    mine_w = to_west[...]
    mine_e = to_east[...]
    lane_of = lambda x, n: x[:, n : n + 1]
    west1[...] = col_step(
        w, pltpu.roll(mine_w, 1, 1), pltpu.roll(w, 1, 1), lane_of(w, 81), lane_of(w, 80),
        lane_of(w, 83), pick_lane(corner_below, 83), lane_of(w, 85),
    )
    east1[...] = col_step(
        e, pltpu.roll(e, 127, 1), pltpu.roll(mine_e, 127, 1), lane_of(e, 80), lane_of(mine_e, 81),
        lane_of(e, 82), pick_lane(corner_below, 82), lane_of(e, 84),
    )


def hot_low(ids):
    grid = row_iota((COLS, ids.shape[1]))
    return jnp.where(grid == (ids & 255), 1.0, 0.0).astype(BF16)


def hot_high(ids, parts, count):
    high = jnp.broadcast_to(ids >> 8, parts.shape)
    return jnp.concatenate([jnp.where(high == h, parts, 0.0) for h in range(count)], axis=0).astype(BF16)


def two_parts(values):
    big = values.astype(BF16).astype(F32)
    return jnp.concatenate([big, values - big], axis=0)


CONTRACT = (((1,), (1,)), ((), ()))


def sweep_body(
    vert, seed, surf, east, north, land, to_east, to_west, west0, east0, send_a, send_b, got_a, got_b,
    weights, slots,
    out, sums, to_north, to_south,
    start0, start1, start2, start3, first0, first1, first2, first3, result, total, coef, side,
    west1, east1, south0, north0, south1, north1, grid_low, arrive, leave,
):
    start = (start0, start1, start2, start3)
    first = (first0, first1, first2, first3)

    def incoming(p, g):
        row = pl.multiple_of(g * 8, 8)
        return pltpu.make_async_copy(
            seed.at[p, :, pl.ds(row, 8), :], start[p].at[:, pl.ds(row + 8, 8), :], arrive.at[p, g]
        )

    def outgoing(g):
        rows = pl.ds(pl.multiple_of(g * 8, 8), 8)
        return pltpu.make_async_copy(result.at[:, :, rows, :], out.at[:, :, rows, :], leave.at[g])

    def fetch(g, carry):
        for p in range(PL):
            incoming(p, g).start()
        return carry

    lax.fori_loop(0, GROUPS, fetch, 0)

    ring(
        vert, to_east, to_west, west0, east0, send_a, send_b, got_a, got_b,
        south0, north0, south1, north1, west1, east1,
    )
    wide = lane_iota((ROWS, COLS))
    tall = row_iota((ROWS, COLS))
    e = east[...]
    n = north[...]
    wet = land[...].astype(F32)
    e_left = jnp.where(wide == 0, west0[:, 81:82], pltpu.roll(e, 1, 1))
    n_below = jnp.where(tall == 0, south0[41:42, :], pltpu.roll(n, 1, 0))
    coef[0] = wet * e
    coef[1] = wet * e_left
    coef[2] = wet * n
    coef[3] = wet * n_below
    coef[4] = wet - wet * (e + e_left + n + n_below)
    coef[5] = wet
    odd = (lane_iota((ROWS, 128)) & 1) == 1
    for i, w, x in ((0, west0, east0), (1, west1, east1)):
        pack = jnp.where(odd, w[...], pltpu.roll(x[...], 2, 1))
        for p in range(PL):
            for k in range(LEV):
                side[i, p, k] = pltpu.roll(pack, (126 - 2 * k - 2 * LEV * p) % 128, 1)
    for p in range(PL):
        for k in range(LEV):
            m = p * LEV + k
            start[p][k, 7:8, :] = south0[m : m + 1, :]
            start[p][k, 136:137, :] = north0[m : m + 1, :]
            first[p][k, 7:8, :] = south1[m : m + 1, :]
            first[p][k, 136:137, :] = north1[m : m + 1, :]
    grid_low[...] = row_iota((COLS, COLS)).astype(F32).astype(BF16)
    which = (row_iota((16, COLS)) >> 3).astype(F32)
    lane = lane_iota((8, 128))
    sub = row_iota((8, 128))
    cs = (slice(0, 128), slice(128, 256))

    def ready(g):
        row = pl.multiple_of(g * 8, 8)
        for p in range(PL):
            incoming(p, g).wait()
        for p in range(PL):
            here = pl.ds(row + 8, 8)
            start[p][0, here, :] = start[p][0, here, :] + surf[p, pl.ds(row, 8), :]

    def stencil(p, g, src, at, c, store):
        row = pl.multiple_of(g * 8, 8)
        here = pl.ds(row + 8, 8)
        below = [None, None]
        u = [src[0, here, cs[t]] for t in range(2)]
        for k in range(LEV):
            edge = side[at, p, k, pl.ds(row, 8), :]
            east_of = [jnp.where(lane == 0, u[1], u[0]), jnp.where(lane == 0, edge, u[1])]
            west_of = [jnp.where(lane == 127, edge, u[0]), jnp.where(lane == 127, u[0], u[1])]
            ahead = [None, None]
            for t in range(2):
                up_rows = src[k, pl.ds(row + 16, 8), cs[t]]
                dn_rows = src[k, pl.ds(row, 8), cs[t]]
                north_u = pltpu.roll(jnp.where(sub == 0, up_rows, u[t]), 7, 0)
                south_u = pltpu.roll(jnp.where(sub == 7, dn_rows, u[t]), 1, 0)
                east_u = pltpu.roll(east_of[t], 127, 1)
                west_u = pltpu.roll(west_of[t], 1, 1)
                new = (
                    c[4][t] * u[t]
                    + c[0][t] * east_u
                    + c[1][t] * west_u
                    + c[2][t] * north_u
                    + c[3][t] * south_u
                )
                flux = None
                if k + 1 < LEV:
                    ahead[t] = src[k + 1, here, cs[t]]
                    flux = vert[k] * (ahead[t] - u[t])
                if flux is None:
                    new = new - c[5][t] * below[t]
                elif below[t] is None:
                    new = new + c[5][t] * flux
                else:
                    new = new + c[5][t] * (flux - below[t])
                below[t] = flux
                store(k, row, t, new)
            u = ahead

    def coefs(g):
        row = pl.multiple_of(g * 8, 8)
        return [[coef[i, pl.ds(row, 8), cs[t]] for t in range(2)] for i in range(6)]

    def step_one(p, g, c):
        def keep(k, row, t, new):
            first[p][k, pl.ds(row + 8, 8), cs[t]] = new

        stencil(p, g, start[p], 0, c, keep)

    def step_two(p, g, c):
        def finish(k, row, t, new):
            result[p, k, pl.ds(row, 8), cs[t]] = new
            if k == 0:
                total[p, pl.ds(row, 8), cs[t]] = new + first[p][0, pl.ds(row + 8, 8), cs[t]]

        stencil(p, g, first[p], 1, c, finish)

    def surfaces(g):
        rows = pl.ds(pl.multiple_of(g * 8, 8), 8)
        return (
            [slots[k, rows, :] for k in range(2)],
            [weights[k, rows, :] for k in range(2)],
            [total[p, rows, :] for p in range(PL)],
        )

    def slot_sums(accs, loaded, lines):
        ids_all, w_all, t_all = loaded
        for r in lines:
            surface = jnp.concatenate([t[r : r + 1, :] for t in t_all], axis=0)
            for k in range(2):
                ids = ids_all[k][r : r + 1, :]
                low = jnp.broadcast_to((ids & 255).astype(F32), (16, COLS)).astype(BF16)
                low = jnp.concatenate([low] * 16, axis=0)
                one_hot = jnp.where(grid_low[...] == low, jnp.array(1, BF16), jnp.array(0, BF16))
                parts = two_parts(surface * w_all[k][r : r + 1, :])
                parts = jnp.concatenate([parts, parts], axis=0).astype(BF16)
                high = (jnp.broadcast_to((ids >> 8).astype(F32), (16, COLS)) - which).astype(BF16)
                hot = jnp.concatenate(
                    [
                        jnp.where(high == jnp.array(2 * h, BF16), parts, jnp.array(0, BF16))
                        for h in range(HPAD // 2)
                    ],
                    axis=0,
                )
                pltpu.matmul_push_rhs(one_hot, r % 2, k, transpose=True)
                pltpu.matmul_acc_lhs(accs[k], hot, load_staged_rhs=r % 2)

    def accumulate(*accs):
        ready(0)
        ready(1)

        def lead(g, carry):
            c = coefs(g)
            ready(g + 2)
            for p in range(PL):
                step_one(p, g, c)
            return carry

        lax.fori_loop(0, 2, lead, 0)
        ready(4)
        c = coefs(0)
        for p in range(PL):
            step_two(p, 0, c)
        c = coefs(2)
        for p in range(PL):
            step_one(p, 2, c)
        outgoing(0).start()

        def body(i, carry):
            @pl.when(i < GROUPS - 2)
            def _():
                ready(i + 2)

            loaded = surfaces(i - 3)
            c_two = coefs(i - 2)
            c_one = coefs(i)
            for p in range(PL):
                slot_sums(accs, loaded, (2 * p, 2 * p + 1))
                step_two(p, i - 2, c_two)
                step_one(p, i, c_one)
            outgoing(i - 2).start()
            return carry

        lax.fori_loop(3, GROUPS, body, 0)

        def trail(g, carry):
            loaded = surfaces(g - 1)
            c = coefs(g)
            for p in range(PL):
                slot_sums(accs, loaded, (2 * p, 2 * p + 1))
                step_two(p, g, c)
            outgoing(g).start()
            return carry

        lax.fori_loop(GROUPS - 2, GROUPS, trail, 0)
        slot_sums(accs, surfaces(GROUPS - 1), range(8))
        summed = pltpu.matmul_pop(accs[0]) + pltpu.matmul_pop(accs[1])
        sums[...] = summed
        to_north[...] = summed[128:136, 128:] + pltpu.roll(summed[128:136, 128:], 4, 0)
        to_south[...] = summed[0:8, :128] + pltpu.roll(summed[0:8, :128], 4, 0)

    pl.run_scoped(accumulate, *[pltpu.ACC(m)((HPAD * 8, COLS), F32) for m in range(2)])

    def drain(g, carry):
        outgoing(g).wait()
        return carry

    lax.fori_loop(0, GROUPS, drain, 0)


def sweep(vert, seed, surf, east, north, land, to_east, to_west, west, east_in, send_a, send_b, got_a, got_b,
          weights, slots):
    whole = lambda *shape: pl.BlockSpec(shape, lambda i: (0,) * len(shape))
    tile = whole(ROWS, COLS)
    cols = whole(ROWS, 128)
    message = whole(4, MSG, 128)
    pair = whole(2, ROWS, COLS)
    anywhere = pl.BlockSpec(memory_space=pl.ANY)
    small = jax.ShapeDtypeStruct((8, 128), F32)
    padded = pltpu.VMEM((LEV, ROWS + 16, COLS), F32)
    return pl.pallas_call(
        sweep_body,
        grid=(1,),
        in_specs=[pl.BlockSpec(memory_space=pltpu.SMEM), anywhere, whole(PL, ROWS, COLS), tile, tile, tile]
        + [cols] * 4
        + [message] * 4
        + [pair] * 2,
        out_specs=[anywhere, whole(HPAD * 8, COLS), whole(8, 128), whole(8, 128)],
        out_shape=[
            jax.ShapeDtypeStruct((PL, LEV, ROWS, COLS), F32),
            jax.ShapeDtypeStruct((HPAD * 8, COLS), F32),
            small,
            small,
        ],
        scratch_shapes=[padded] * 8
        + [
            pltpu.VMEM((PL, LEV, ROWS, COLS), F32),
            pltpu.VMEM((PL, ROWS, COLS), F32),
            pltpu.VMEM((6, ROWS, COLS), F32),
            pltpu.VMEM((2, PL, LEV, ROWS, 128), F32),
            pltpu.VMEM((ROWS, 128), F32),
            pltpu.VMEM((ROWS, 128), F32),
        ]
        + [pltpu.VMEM((MSG, COLS), F32)] * 4
        + [
            pltpu.VMEM((COLS, COLS), BF16),
            pltpu.SemaphoreType.DMA((PL, GROUPS)),
            pltpu.SemaphoreType.DMA((GROUPS,)),
        ],
        compiler_params=VM,
        name="sweep",
    )(vert, seed, surf, east, north, land, to_east, to_west, west, east_in, send_a, send_b, got_a, got_b,
      weights, slots)


def gather_body(sums, south, north, serve, out):
    lane = lane_iota((PL, COLS))
    acc = jnp.zeros((128, COLS), F32)
    for h in range(HI):
        tile = sums[8 * h : 8 * h + 8, :]
        values = tile[0:4, :] + tile[4:8, :]
        if h == 0:
            values = jnp.where(lane < 128, jnp.concatenate([south[0:4, :], south[0:4, :]], axis=1), values)
        if h == HI - 1:
            values = jnp.where(lane >= 128, jnp.concatenate([north[0:4, :], north[0:4, :]], axis=1), values)
        ids = serve[:, COLS * h : COLS * h + COLS]
        acc = acc + lax.dot_general(
            hot_high(ids, two_parts(values), 16), hot_low(ids), CONTRACT, preferred_element_type=F32
        )
    for h in range(16):
        tile = acc[8 * h : 8 * h + 8, :]
        values = tile[0:4, :] + tile[4:8, :]
        for p in range(PL):
            for t in range(2):
                out[p, 2 * h + t : 2 * h + t + 1, :] = values[p : p + 1, 128 * t : 128 * t + 128]


def gather(sums, south, north, serve):
    whole = lambda *shape: pl.BlockSpec(shape, lambda i: (0,) * len(shape))
    return pl.pallas_call(
        gather_body,
        grid=(1,),
        in_specs=[whole(HPAD * 8, COLS), whole(8, 128), whole(8, 128), whole(1, LISTS * 128)],
        out_specs=whole(PL, 32, 128),
        out_shape=jax.ShapeDtypeStruct((PL, 32, 128), F32),
        compiler_params=VM,
        name="gather",
    )(sums, south, north, serve)


def ladder(lon_count, lat_count, shift):
    place = lambda a, j: j * lat_count + a
    pairs = []
    for j in range(lon_count):
        for a in range(1, lat_count - 1, 2):
            pairs.append((place(a, j), place(a + 1, j)))
            pairs.append((place(a + 1, j), place(a, j)))
        pairs.append((place(lat_count - 1, j), place(lat_count - 1, (shift - 1 - j) % lon_count)))
    return pairs


def shards(
    ocean_seed, forcing_pert, land_mask, east_coef, north_coef, vert_coef, remap_weight, ocean_slots,
    serve_cells, fold_map,
):
    lat_count = lax.axis_size("lat")
    lon_count = lax.axis_size("lon")
    upward = [(i, i + 1) for i in range(lat_count - 1)]
    downward = [(i + 1, i) for i in range(lat_count - 1)]
    eastward = [(i, (i + 1) % lon_count) for i in range(lon_count)]
    westward = [((i + 1) % lon_count, i) for i in range(lon_count)]

    cells = serve_cells.reshape(-1)

    def list_message(row, ids):
        return jnp.concatenate([row, ids.astype(F32)[None], jnp.zeros((3, 128), F32)], axis=0)

    south_list = lax.ppermute(list_message(forcing_pert[:, -1], cells[-128:]), "lat", upward)
    north_list = lax.ppermute(list_message(forcing_pert[:, 0], cells[:128]), "lat", downward)

    shift = ((fold_map[0] + 1) // COLS) % lon_count
    shift, forcing = lax.optimization_barrier((shift, forcing_pert))

    surf, to_east, to_west, send_a, send_b = pick(
        forcing, serve_cells, south_list, north_list, ocean_slots, remap_weight,
        ocean_seed, east_coef, north_coef, land_mask,
    )

    west = lax.ppermute(to_east, "lon", eastward)
    east = lax.ppermute(to_west, "lon", westward)
    send_a, send_b = corners(west, east, send_a, send_b)
    got_a = lax.ppermute(send_a, "lat", [(i ^ 1, i) for i in range(lat_count)])
    got_b = lax.switch(
        shift,
        [
            lambda v, s=s: lax.ppermute(v, ("lon", "lat"), ladder(lon_count, lat_count, s))
            for s in range(lon_count)
        ],
        send_b,
    )
    adjoint_two, sums, to_north, to_south = sweep(
        vert_coef, ocean_seed, surf, east_coef, north_coef, land_mask, to_east, to_west, west, east,
        send_a, send_b, got_a, got_b, remap_weight, ocean_slots,
    )
    from_south = lax.ppermute(to_north, "lat", upward)
    from_north = lax.ppermute(to_south, "lat", downward)
    stress_sens = gather(sums, from_south, from_north, serve_cells)
    return (adjoint_two, stress_sens)


def solution(mesh):
    return jax.shard_map(
        shards,
        mesh=mesh,
        in_specs=(
            P(None, None, "lat", "lon"),
            P(None, "lat", "lon"),
            P("lat", "lon"),
            P("lat", "lon"),
            P("lat", "lon"),
            P(),
            P(None, "lat", "lon"),
            P(None, "lat", "lon"),
            P("lat", "lon"),
            P(),
        ),
        out_specs=(P(None, None, "lat", "lon"), P(None, "lat", "lon")),
        check_vma=False,
    )
```
